32 devices in a mesh: groups: 2 (over y), expert: 8 (over z, x), tensor: 2 (over core).
Axes of the slice: x: 2, y: 2, z: 4, core: 2. Of those that a mesh axis runs over, the one named last changes fastest.
Arguments:
- tokens: bfloat16 [2, 1024, 2048], P(None, ('groups', 'expert')), parts along dimension 1, may hold values from -6 to 6
- routes: int32 [2, 1024, 8], P(None, ('groups', 'expert')), parts along dimension 1, may hold values from 0 to 7, as said below
- probs: float32 [2, 1024, 8], P(None, ('groups', 'expert')), parts along dimension 1, may hold values from 0.02 to 0.3
- up_weight: bfloat16 [8, 2048, 768], P('expert', None, 'tensor'), may hold values from -0.125 to 0.125
- down_weight: bfloat16 [8, 768, 2048], P('expert', None, 'tensor'), may hold values from -0.21875 to 0.21875
- old_place: int32 [16], P('groups'), parts along dimension 0, may hold values from 0 to 7, as said below
- new_place: int32 [32], P('groups'), parts along dimension 0, may hold values from 0 to 7, as said below
Outputs:
- mixed: bfloat16 [2, 1024, 2048], P(None, ('groups', 'expert'), 'tensor'), parts along dimension 1
- slot_rows: int32 [32], P(('groups', 'expert')), parts along dimension 0
The draws below stay inside these ranges and needn't reach their ends.
There are 2 independent parts, one for each index of `groups`. The reference program is written for one: setup_inputs(seed, part) draws one part's arguments, and reference() takes and returns one part's arrays. A program takes and returns all parts, laid end to end along the dimension named above; an argument that names none is the same for every part. Nothing has to cross between parts.
Inputs may be any that keep to these rules, and one draw needn't show every extreme that they name: `routes`: each token names 8 different experts. `old_place`: each expert is held by exactly one old slot. `new_place`: new slot 2 * s holds the expert of old slot s; no expert is held by more than 4 new slots, and some expert by exactly 4.
All inputs are finite; a program needn't handle non-finite values.
Results may differ from the reference program's by a relative error of at most 0.0058.
Values may be sent and summed in bfloat16 or wider, within the bound.
No kernel may reach another device: no remote copies, remote signals or barrier semaphores. Data moves between devices by JAX's collectives and lax.ppermute only.
A program may use at most 128 MiB of HBM per device.

```python
import math
import jax
import jax.numpy as jnp
from jax import lax

D = 2048
FF = 768
TOPK = 8
MB = 2
REPLICAS = 4
TOK_DEV = 64
EXPERTS = 8
SLOTS = 16
TOKENS = 512
CAPACITY = 64
SLOT_CAP = 40
N_EXPERT = 8


def popularity(key):
    return jax.random.permutation(jax.random.fold_in(key, 7001), EXPERTS).astype(jnp.int32)


def draw_old_place(key, part):
    return jax.random.permutation(jax.random.fold_in(key, 7002), EXPERTS).astype(jnp.int32)


def draw_new_place(key, part):
    old_place = draw_old_place(key, part)
    order = popularity(key)
    eighth = EXPERTS // 8
    spots = jnp.arange(EXPERTS, dtype=jnp.int32)
    middle = eighth + (spots - 3 * eighth) // 2
    tail = 2 * eighth + (spots - 5 * eighth)
    rank_pick = jnp.where(spots < 3 * eighth, spots // 3, jnp.where(spots < 5 * eighth, middle, tail))
    extras = order[rank_pick]
    extras = jax.random.permutation(jax.random.fold_in(key, 7003), extras)
    return jnp.stack([old_place, extras], axis=1).reshape(-1).astype(jnp.int32)


def draw_routes(key, part):
    order = popularity(key)
    rank_of = jnp.zeros((EXPERTS,), jnp.int32).at[order].set(jnp.arange(EXPERTS, dtype=jnp.int32))
    eighth = EXPERTS // 8
    bias = jnp.where(rank_of < eighth, 14418, jnp.where(rank_of < 2 * eighth, 3932, 0)).astype(jnp.int32)
    noise = jax.random.randint(jax.random.fold_in(key, 7004), (MB, TOKENS, EXPERTS), 0, 65536, dtype=jnp.int32)
    labels = jnp.arange(EXPERTS, dtype=jnp.int32)
    scores = (noise + bias[None, None, :]) * EXPERTS + labels[None, None, :]
    picked = lax.top_k(scores, TOPK)[1]
    return picked.astype(jnp.int32)


def shard_levels(key, extent, cuts, least, largest):
    factor_of, own = 1.0, jax.random.fold_in(key, 6)
    for position, parts in cuts:
        steps = jnp.exp(jax.random.uniform(jax.random.fold_in(own, position), (parts,), jnp.float32, least / len(cuts), largest / len(cuts)))
        factor_of = factor_of * jnp.repeat(steps, extent[position] // parts).reshape([-1 if axis == position else 1 for axis in range(len(extent))])
    return factor_of


def normal_values(rng, dims, deviation, reach, split=(), held_as=jnp.bfloat16):
    values = deviation * jax.random.normal(rng, dims, jnp.float32)
    if split:
        values = values * shard_levels(rng, dims, split, -0.22, 0.18)
    return jnp.clip(values, -reach, reach).astype(held_as)


def setup_inputs(seed: int = 0, part: int = 0) -> dict:
    key_list = jax.random.split(jax.random.key(seed), 8)
    part_keys = jax.random.split(jax.random.fold_in(key_list[7], part), 8)
    tokens = normal_values(part_keys[0], (MB, TOKENS, D), 1.0, 6.0, ((1, 8),))
    routes = draw_routes(jax.random.fold_in(jax.random.fold_in(key_list[7], part), 71), part)
    probs = jnp.clip(jnp.exp(math.log(0.3) - 2.7080503 * jax.random.uniform(part_keys[2], (MB, TOKENS, TOPK), jnp.float32) ** shard_levels(part_keys[2], (MB, TOKENS, TOPK), ((1, 8),), -0.2, 0.2)), 0.02, 0.3)
    up_weight = normal_values(key_list[3], (EXPERTS, D, FF), D ** -0.5, 0.125, ((0, 8), (2, 2)))
    down_weight = normal_values(key_list[4], (EXPERTS, FF, D), FF ** -0.5, 0.21875, ((0, 8), (2, 2)))
    old_place = draw_old_place(jax.random.fold_in(jax.random.fold_in(key_list[7], part), 71), part)
    new_place = draw_new_place(jax.random.fold_in(jax.random.fold_in(key_list[7], part), 71), part)
    return dict(tokens=tokens, routes=routes, probs=probs, up_weight=up_weight, down_weight=down_weight, old_place=old_place, new_place=new_place)


def block_ranks(labels):
    positions = jnp.arange(labels.shape[1]).astype(jnp.int32)
    earlier = positions[None, :] < positions[:, None]

    def one_block(row):
        same_label = row[:, None] == row[None, :]
        return jnp.sum((same_label & earlier).astype(jnp.int32), axis=1).astype(jnp.int32)

    return lax.map(one_block, labels)


def expert_rows(tokens_mb, probs_mb, routes_mb, kept, up_weight, down_weight, old_place, bound):
    flat_routes = routes_mb.reshape(-1)
    flat_kept = kept.reshape(-1)
    flat_probs = probs_mb.reshape(-1)
    row_total = flat_routes.shape[0]

    def one_slot(total, slot_items):
        up_mat, down_mat, expert_id = slot_items
        wanted = (flat_routes == expert_id) & flat_kept
        chosen = jnp.nonzero(wanted, size=bound, fill_value=row_total)[0].astype(jnp.int32)
        safe = jnp.minimum(chosen, row_total - 1)
        token_ids = safe // TOPK
        hidden = jax.nn.silu(jnp.dot(tokens_mb[token_ids], up_mat, preferred_element_type=jnp.float32)).astype(jnp.bfloat16)
        rounded = jnp.dot(hidden, down_mat, preferred_element_type=jnp.float32).astype(jnp.bfloat16)
        outputs = lax.optimization_barrier(rounded).astype(jnp.float32)
        scales = jnp.where(chosen < row_total, flat_probs[safe], jnp.zeros_like(flat_probs[safe]))
        return total.at[token_ids].add(outputs * scales[:, None]), None

    start = jnp.zeros((tokens_mb.shape[0], D), jnp.float32)
    total, unused = lax.scan(one_slot, start, (up_weight, down_weight, old_place))
    return total.astype(jnp.bfloat16)


def reference(tokens, routes, probs, up_weight, down_weight, old_place, new_place):
    slot_ids = jnp.arange(EXPERTS).astype(jnp.int32)
    home = jnp.zeros((EXPERTS,), jnp.int32).at[old_place].set(slot_ids)
    early_blocks = routes[0].reshape(N_EXPERT, TOK_DEV * TOPK)
    early_kept = block_ranks(home[early_blocks]) < CAPACITY
    later_blocks = routes[1].reshape(N_EXPERT, TOK_DEV * TOPK)
    new_ids = jnp.arange(SLOTS).astype(jnp.int32)
    same_slot = new_place[:, None] == new_place[None, :]
    occurrence = jnp.sum((same_slot & (new_ids[None, :] < new_ids[:, None])).astype(jnp.int32), axis=1).astype(jnp.int32)
    replicas = jnp.zeros((EXPERTS,), jnp.int32).at[new_place].add(jnp.ones((SLOTS,), jnp.int32))
    table = jnp.zeros((EXPERTS, REPLICAS), jnp.int32).at[new_place, occurrence].set(new_ids)
    sources = jnp.arange(N_EXPERT).astype(jnp.int32)[:, None]
    wanted = (block_ranks(later_blocks) + sources) % replicas[later_blocks]
    later_slots = table[later_blocks, wanted]
    later_kept = block_ranks(later_slots) < SLOT_CAP
    early_out = expert_rows(tokens[0], probs[0], routes[0], early_kept, up_weight, down_weight, old_place, N_EXPERT * CAPACITY)
    later_bound = N_EXPERT * min(REPLICAS * SLOT_CAP, TOK_DEV)
    later_out = expert_rows(tokens[1], probs[1], routes[1], later_kept, up_weight, down_weight, old_place, later_bound)
    slot_rows = jnp.zeros((SLOTS,), jnp.int32).at[later_slots.reshape(-1)].add(jnp.ones((N_EXPERT * TOK_DEV * TOPK,), jnp.int32))
    return jnp.stack([early_out, later_out]), slot_rows
```

```python
import functools

import jax
import jax.numpy as jnp
from jax import lax
from jax.experimental import pallas as pl
from jax.experimental.pallas import tpu as pltpu
from jax.sharding import PartitionSpec as P

REPLICAS = 4
LANES = 128


def earlier_same(labels):
    positions = jnp.arange(labels.shape[0], dtype=jnp.int32)
    earlier = positions[None, :] < positions[:, None]
    same_label = labels[:, None] == labels[None, :]
    return jnp.sum((earlier & same_label).astype(jnp.int32), axis=1)


def holder_index(labels, holders):
    matches = labels[:, None] == holders[None, :]
    positions = jnp.arange(holders.shape[0], dtype=jnp.int32)
    return jnp.sum(matches.astype(jnp.int32) * positions[None, :], axis=1)


def replica_slots(flat_routes, new_place, source_index):
    positions = jnp.arange(new_place.shape[0], dtype=jnp.int32)
    same_slot = new_place[:, None] == new_place[None, :]
    occurrence = jnp.sum(
        (same_slot & (positions[None, :] < positions[:, None])).astype(jnp.int32), axis=1
    )
    matches = flat_routes[:, None] == new_place[None, :]
    replicas = jnp.sum(matches.astype(jnp.int32), axis=1)
    wanted = (earlier_same(flat_routes) + source_index) % replicas
    chosen = matches & (occurrence[None, :] == wanted[:, None])
    slot_ids = jnp.sum(chosen.astype(jnp.int32) * positions[None, :], axis=1)
    return (slot_ids, chosen)


def capacity_for(block_rows, targets, token_count):
    return min(token_count, max(2, (5 * block_rows + 4 * targets - 1) // (4 * targets)))


def serve_cells(tokens_mb, probs_mb, cell_ids, target_count, block, up_local, down_local):
    token_count = tokens_mb.shape[0]
    topk_count = cell_ids.shape[0] // token_count
    slots_here = up_local.shape[0]
    cells = jnp.arange(target_count * block, dtype=jnp.int32)
    placed = (cells[:, None] == cell_ids[None, :]).astype(jnp.bfloat16)
    by_token = jnp.sum(placed.reshape(target_count * block, token_count, topk_count), axis=2)
    send_rows = jnp.dot(by_token, tokens_mb, preferred_element_type=jnp.float32).astype(
        jnp.bfloat16
    )
    send_rows = send_rows.reshape(target_count, block, -1)
    received = lax.all_to_all(send_rows, "expert", split_axis=0, concat_axis=0, tiled=True)
    sources = received.shape[0] // slots_here
    grid = received.reshape(sources, slots_here, received.shape[1], received.shape[2])
    hidden = jax.nn.silu(
        jnp.einsum("nscd,sdf->nscf", grid, up_local, preferred_element_type=jnp.float32)
    ).astype(jnp.bfloat16)
    hidden = lax.all_gather(hidden, "tensor", axis=3, tiled=True)
    outputs = jnp.einsum(
        "nscf,sfd->nscd", hidden, down_local, preferred_element_type=jnp.float32
    ).astype(jnp.bfloat16)
    outputs = outputs.reshape(received.shape[0], received.shape[1], -1)
    returned = lax.all_to_all(outputs, "expert", split_axis=0, concat_axis=0, tiled=True)
    flat_back = returned.reshape(target_count * block, -1)
    picked = lax.dot_general(
        placed, flat_back, (((0,), (0,)), ((), ())), preferred_element_type=jnp.float32
    )
    weighted = picked.reshape(token_count, topk_count, -1) * probs_mb[:, :, None]
    return jnp.sum(weighted, axis=1).astype(jnp.bfloat16)


def by_capacity(tokens, routes, probs, up_weight, down_weight, old_place, new_place):
    source_index = lax.axis_index("expert")
    devices = lax.axis_size("expert")
    token_count = tokens.shape[1]
    topk_count = routes.shape[2]
    block_rows = token_count * topk_count
    expert_count = old_place.shape[0]
    slot_count = new_place.shape[0]
    early_cap = capacity_for(block_rows, expert_count, token_count)
    later_cap = capacity_for(block_rows, slot_count, token_count)
    early_routes = routes[0].reshape(-1)
    later_routes = routes[1].reshape(-1)
    early_slots = holder_index(early_routes, old_place)
    early_rank = earlier_same(early_slots)
    early_cells = jnp.where(early_rank < early_cap, early_slots * early_cap + early_rank, -1)
    later_slots, chosen = replica_slots(later_routes, new_place, source_index)
    slot_counts = lax.psum(jnp.sum(chosen.astype(jnp.int32), axis=0), "expert")
    slot_dev = slot_count // devices
    slot_rows = lax.dynamic_slice_in_dim(slot_counts, source_index * slot_dev, slot_dev, 0)
    later_rank = earlier_same(later_slots)
    later_kept = later_rank < later_cap
    early_out = serve_cells(
        tokens[0], probs[0], early_cells, expert_count, early_cap, up_weight, down_weight
    )
    homes = holder_index(later_routes, old_place)
    home_block = min(token_count, REPLICAS * later_cap)
    home_labels = jnp.where(later_kept, homes, -1)
    home_rank = earlier_same(home_labels)
    later_cells = jnp.where(later_kept, homes * home_block + home_rank, -1)
    later_out = serve_cells(
        tokens[1], probs[1], later_cells, expert_count, home_block, up_weight, down_weight
    )
    return (jnp.stack([early_out, later_out]), slot_rows)


def ring_order(mesh):
    line = mesh.devices[0, :, 0]
    count = len(line)
    if count > 16 or not all(hasattr(d, "coords") for d in line):
        return tuple(range(count))
    spots = [tuple(d.coords) for d in line]

    def near(a, b):
        return sum(abs(i - j) for i, j in zip(spots[a], spots[b])) == 1

    def extend(path):
        if len(path) == count:
            return path if near(path[-1], path[0]) else None
        for spot in range(count):
            if spot not in path and near(path[-1], spot):
                if found := extend(path + [spot]):
                    return found
        return None

    return tuple(extend([0]) or range(count))


def token_weights(routes, probs, old_place, new_place):
    token_count, topk_count = routes.shape[1], routes.shape[2]
    block_rows = token_count * topk_count
    early_cap = capacity_for(block_rows, old_place.shape[0], token_count)
    later_cap = capacity_for(block_rows, new_place.shape[0], token_count)
    holders = jnp.sum((old_place[:, None] == new_place[None, :]).astype(jnp.int32), axis=1)
    served = jnp.stack([jnp.full_like(holders, early_cap), later_cap * holders])
    tokens = jnp.arange(token_count, dtype=jnp.int32)
    named = routes[:, :, :, None] == old_place[None, None, None, :]
    weights = jnp.sum(jnp.where(named, probs[:, :, :, None], 0.0), axis=2)
    return jnp.where(tokens[None, :, None] < served[:, None, :], weights, 0.0)


def own_slot_rows(new_place, source_index, devices, token_count):
    slot_count = new_place.shape[0]
    slot_dev = slot_count // devices
    positions = jnp.arange(slot_count, dtype=jnp.int32)
    same_slot = new_place[:, None] == new_place[None, :]
    occurrence = jnp.sum(
        (same_slot & (positions[None, :] < positions[:, None])).astype(jnp.int32), axis=1
    )
    holders = jnp.sum(same_slot.astype(jnp.int32), axis=1)
    turns = (
        jnp.arange(devices, dtype=jnp.int32)[:, None]
        + jnp.arange(token_count, dtype=jnp.int32)[None, :]
    ).reshape(-1)
    taken = lax.rem(turns[None, :], holders[:, None] + 0 * turns[None, :]) == occurrence[:, None]
    counts = jnp.sum(taken.astype(jnp.int32), axis=1)
    return lax.dynamic_slice_in_dim(counts, source_index * slot_dev, slot_dev, 0)


def expert_kernel(chunks, width, experts, *refs):
    place, refs = refs[0], refs[1:]
    rows, refs = refs[:chunks], refs[chunks:]
    (up_own, up_pair, down_own, down_pair), refs = refs[:4], refs[4:]
    outs, refs = refs[:chunks], refs[chunks:]
    x_buf, up_a, up_b, down_a, down_b, sems = refs
    copies = [
        pltpu.make_async_copy(src, dst, sems.at[i])
        for i, (src, dst) in enumerate(
            ((up_own, up_a), (up_pair, up_b), (down_own, down_a), (down_pair, down_b))
        )
    ]
    for copy in copies:
        copy.start()
    slot, core = place[0], place[1]
    size = rows[0].shape[0]
    lane = lax.broadcasted_iota(jnp.int32, (size, rows[0].shape[1] - width), 1)
    mine = (lane == slot) | (lane == experts + slot)
    scales = []
    for i, row in enumerate(rows):
        x_buf[i * size : (i + 1) * size, :] = row[:, :width]
        side = row[:, width:].astype(jnp.float32)
        scales.append(jnp.sum(jnp.where(mine, side, 0.0), axis=1, keepdims=True))
    scale = jnp.concatenate(scales, axis=0)
    x = x_buf[...]
    parts = []
    for copy, up in zip(copies[:2], (up_a, up_b)):
        copy.wait()
        v = jnp.dot(x, up[...], preferred_element_type=jnp.float32)
        parts.append((v / (1.0 + jnp.exp(-v))).astype(jnp.bfloat16))
    first = jnp.where(core == 0, parts[0], parts[1])
    second = jnp.where(core == 0, parts[1], parts[0])
    hidden = jnp.concatenate([first, second], axis=1)
    half = down_a.shape[1]
    for j, (copy, down) in enumerate(zip(copies[2:], (down_a, down_b))):
        copy.wait()
        y = jnp.dot(hidden, down[...], preferred_element_type=jnp.float32)
        y = y.astype(jnp.bfloat16).astype(jnp.float32) * scale
        for i, out in enumerate(outs):
            out[:, j * half : (j + 1) * half] = y[i * size : (i + 1) * size].astype(out.dtype)


def expert_rows(place, rows, weights, width, experts, out_types):
    chunks, size = len(rows), rows[0].shape[0]
    up, down = weights[0], weights[2]
    total = chunks * size
    flops = 2 * total * width * 4 * up.shape[1]
    vmem = pl.BlockSpec(memory_space=pltpu.VMEM)
    return pl.pallas_call(
        functools.partial(expert_kernel, chunks, width, experts),
        out_shape=[jax.ShapeDtypeStruct((size, width), t) for t in out_types],
        in_specs=[pl.BlockSpec(memory_space=pltpu.SMEM)]
        + [vmem] * chunks
        + [pl.BlockSpec(memory_space=pl.ANY)] * 4,
        out_specs=[vmem] * chunks,
        scratch_shapes=[
            pltpu.VMEM((total, width), jnp.bfloat16),
            pltpu.VMEM(up.shape, up.dtype),
            pltpu.VMEM(up.shape, up.dtype),
            pltpu.VMEM(down.shape, down.dtype),
            pltpu.VMEM(down.shape, down.dtype),
            pltpu.SemaphoreType.DMA((4,)),
        ],
        compiler_params=pltpu.CompilerParams(vmem_limit_bytes=24 << 20),
        cost_estimate=pl.CostEstimate(
            flops=flops,
            bytes_accessed=4 * (up.size + down.size) + 8 * total * width,
            transcendentals=2 * total * up.shape[1],
        ),
    )(place, *rows, *weights)


def by_ring(ring, tokens, routes, probs, up_weight, down_weight, old_place, new_place):
    core = lax.axis_index("tensor")
    source_index = lax.axis_index("expert")
    devices = lax.axis_size("expert")
    token_count, width = tokens.shape[1], tokens.shape[2]
    experts = old_place.shape[0]
    both = ("expert", "tensor")
    steps = devices // 2
    ahead = []
    for spot, here in enumerate(ring):
        there = ring[(spot + 1) % devices]
        ahead += [(2 * here, 2 * there), (2 * there + 1, 2 * here + 1)]
    back = [(b, a) for a, b in ahead]
    swap = [(0, 1), (1, 0)]

    scales = token_weights(routes, probs, old_place, new_place)
    high = lax.reduce_precision(scales, exponent_bits=8, mantissa_bits=7)
    side = jnp.concatenate([high, scales - high], axis=2).astype(jnp.bfloat16)
    lanes = -(-2 * experts // LANES) * LANES
    side = jnp.pad(side, ((0, 0), (0, 0), (0, lanes - 2 * experts)))
    packed = jnp.concatenate([tokens, side], axis=2)
    own = [
        lax.dynamic_index_in_dim(packed, core, 0, keepdims=False),
        lax.dynamic_index_in_dim(packed, 1 - core, 0, keepdims=False),
    ]
    first, second = [own[0]], [own[1]]
    for step in range(1, steps + 1):
        first.append(lax.ppermute(first[-1], both, ahead))
        if step < steps:
            second.append(lax.ppermute(second[-1], both, ahead))
    up_own, down_own = up_weight[0], down_weight[0]
    up_pair = lax.ppermute(up_own, "tensor", swap)
    down_pair = lax.ppermute(down_own, "tensor", swap)
    weights = (up_own, up_pair, down_own, down_pair)
    place = jnp.stack([source_index, core]).astype(jnp.int32)
    run = functools.partial(
        expert_rows, place, weights=weights, width=width, experts=experts
    )
    f32, bf16 = jnp.float32, jnp.bfloat16
    part_first, part_second = [None] * (steps + 1), [None] * steps
    part_first[0], part_first[1], part_second[1] = run(
        rows=[first[0], first[1], second[1]], out_types=[f32] * 3
    )
    for step in range(2, steps):
        part_first[step], part_second[step] = run(
            rows=[first[step], second[step]],
            out_types=[f32, bf16 if step == steps - 1 else f32],
        )
    (part_first[steps],) = run(rows=[first[steps]], out_types=[bf16])

    sum_first, sum_second = part_first[steps], part_second[steps - 1]
    for step in range(steps - 1, -1, -1):
        sum_first = lax.ppermute(sum_first, both, back)
        sum_first = part_first[step] + sum_first.astype(f32)
        if step > 0:
            sum_first = sum_first.astype(bf16)
        if step < steps - 1:
            sum_second = lax.ppermute(sum_second, both, back)
            if step > 0:
                sum_second = (part_second[step] + sum_second.astype(f32)).astype(bf16)
    half = width // 2
    from_second = lax.ppermute(sum_second[:, half:], "tensor", swap)
    from_first = lax.ppermute(sum_first[:, half:].astype(bf16), "tensor", swap)
    own_batch = sum_first[:, :half] + from_second.astype(f32)
    pair_batch = sum_second[:, :half].astype(f32) + from_first.astype(f32)
    batch = jnp.arange(2, dtype=jnp.int32)[:, None, None]
    mixed = jnp.where(batch == core, own_batch[None], pair_batch[None]).astype(bf16)
    return (mixed, own_slot_rows(new_place, source_index, devices, token_count))


def on_device(ring, tokens, routes, probs, up_weight, down_weight, old_place, new_place):
    devices = lax.axis_size("expert")
    experts = old_place.shape[0]
    arrays = (tokens, routes, probs, up_weight, down_weight, old_place, new_place)
    if (
        experts == routes.shape[2]
        and experts == devices
        and devices >= 6
        and devices % 2 == 0
        and lax.axis_size("tensor") == 2
        and tokens.shape[0] == 2
    ):
        return by_ring(ring, *arrays)
    return by_capacity(*arrays)


def solution(mesh):
    placed = (
        P(None, ("groups", "expert"), None),
        P(None, ("groups", "expert"), None),
        P(None, ("groups", "expert"), None),
        P("expert", None, "tensor"),
        P("expert", None, "tensor"),
        P("groups"),
        P("groups"),
    )
    return jax.shard_map(
        functools.partial(on_device, ring_order(mesh)),
        mesh=mesh,
        in_specs=placed,
        out_specs=(P(None, ("groups", "expert"), "tensor"), P(("groups", "expert"))),
        check_vma=False,
    )
```

```python
import functools

import jax
import jax.numpy as jnp
from jax import lax
from jax.experimental import pallas as pl
from jax.experimental.pallas import tpu as pltpu
from jax.sharding import PartitionSpec as P

REPLICAS = 4
LANES = 128
VMEM_BYTES = 67043328


def earlier_same(labels):
    positions = jnp.arange(labels.shape[0], dtype=jnp.int32)
    earlier = positions[None, :] < positions[:, None]
    same_label = labels[:, None] == labels[None, :]
    return jnp.sum((earlier & same_label).astype(jnp.int32), axis=1)


def holder_index(labels, holders):
    matches = labels[:, None] == holders[None, :]
    positions = jnp.arange(holders.shape[0], dtype=jnp.int32)
    return jnp.sum(matches.astype(jnp.int32) * positions[None, :], axis=1)


def replica_slots(flat_routes, new_place, source_index):
    positions = jnp.arange(new_place.shape[0], dtype=jnp.int32)
    same_slot = new_place[:, None] == new_place[None, :]
    occurrence = jnp.sum(
        (same_slot & (positions[None, :] < positions[:, None])).astype(jnp.int32), axis=1
    )
    matches = flat_routes[:, None] == new_place[None, :]
    replicas = jnp.sum(matches.astype(jnp.int32), axis=1)
    wanted = (earlier_same(flat_routes) + source_index) % replicas
    chosen = matches & (occurrence[None, :] == wanted[:, None])
    slot_ids = jnp.sum(chosen.astype(jnp.int32) * positions[None, :], axis=1)
    return (slot_ids, chosen)


def capacity_for(block_rows, targets, token_count):
    return min(token_count, max(2, (5 * block_rows + 4 * targets - 1) // (4 * targets)))


def serve_cells(tokens_mb, probs_mb, cell_ids, target_count, block, up_local, down_local):
    token_count = tokens_mb.shape[0]
    topk_count = cell_ids.shape[0] // token_count
    slots_here = up_local.shape[0]
    cells = jnp.arange(target_count * block, dtype=jnp.int32)
    placed = (cells[:, None] == cell_ids[None, :]).astype(jnp.bfloat16)
    by_token = jnp.sum(placed.reshape(target_count * block, token_count, topk_count), axis=2)
    send_rows = jnp.dot(by_token, tokens_mb, preferred_element_type=jnp.float32).astype(
        jnp.bfloat16
    )
    send_rows = send_rows.reshape(target_count, block, -1)
    received = lax.all_to_all(send_rows, "expert", split_axis=0, concat_axis=0, tiled=True)
    sources = received.shape[0] // slots_here
    grid = received.reshape(sources, slots_here, received.shape[1], received.shape[2])
    hidden = jax.nn.silu(
        jnp.einsum("nscd,sdf->nscf", grid, up_local, preferred_element_type=jnp.float32)
    ).astype(jnp.bfloat16)
    hidden = lax.all_gather(hidden, "tensor", axis=3, tiled=True)
    outputs = jnp.einsum(
        "nscf,sfd->nscd", hidden, down_local, preferred_element_type=jnp.float32
    ).astype(jnp.bfloat16)
    outputs = outputs.reshape(received.shape[0], received.shape[1], -1)
    returned = lax.all_to_all(outputs, "expert", split_axis=0, concat_axis=0, tiled=True)
    flat_back = returned.reshape(target_count * block, -1)
    picked = lax.dot_general(
        placed, flat_back, (((0,), (0,)), ((), ())), preferred_element_type=jnp.float32
    )
    weighted = picked.reshape(token_count, topk_count, -1) * probs_mb[:, :, None]
    return jnp.sum(weighted, axis=1).astype(jnp.bfloat16)


def by_capacity(tokens, routes, probs, up_weight, down_weight, old_place, new_place):
    source_index = lax.axis_index("expert")
    devices = lax.axis_size("expert")
    token_count = tokens.shape[1]
    topk_count = routes.shape[2]
    block_rows = token_count * topk_count
    expert_count = old_place.shape[0]
    slot_count = new_place.shape[0]
    early_cap = capacity_for(block_rows, expert_count, token_count)
    later_cap = capacity_for(block_rows, slot_count, token_count)
    early_routes = routes[0].reshape(-1)
    later_routes = routes[1].reshape(-1)
    early_slots = holder_index(early_routes, old_place)
    early_rank = earlier_same(early_slots)
    early_cells = jnp.where(early_rank < early_cap, early_slots * early_cap + early_rank, -1)
    later_slots, chosen = replica_slots(later_routes, new_place, source_index)
    slot_counts = lax.psum(jnp.sum(chosen.astype(jnp.int32), axis=0), "expert")
    slot_dev = slot_count // devices
    slot_rows = lax.dynamic_slice_in_dim(slot_counts, source_index * slot_dev, slot_dev, 0)
    later_rank = earlier_same(later_slots)
    later_kept = later_rank < later_cap
    early_out = serve_cells(
        tokens[0], probs[0], early_cells, expert_count, early_cap, up_weight, down_weight
    )
    homes = holder_index(later_routes, old_place)
    home_block = min(token_count, REPLICAS * later_cap)
    home_labels = jnp.where(later_kept, homes, -1)
    home_rank = earlier_same(home_labels)
    later_cells = jnp.where(later_kept, homes * home_block + home_rank, -1)
    later_out = serve_cells(
        tokens[1], probs[1], later_cells, expert_count, home_block, up_weight, down_weight
    )
    return (jnp.stack([early_out, later_out]), slot_rows)


def ring_order(mesh):
    line = mesh.devices[0, :, 0]
    count = len(line)
    if count > 16 or not all(hasattr(d, "coords") for d in line):
        return tuple(range(count))
    spots = [tuple(d.coords) for d in line]

    def near(a, b):
        return sum(abs(i - j) for i, j in zip(spots[a], spots[b])) == 1

    def extend(path):
        if len(path) == count:
            return path if near(path[-1], path[0]) else None
        for spot in range(count):
            if spot not in path and near(path[-1], spot):
                if found := extend(path + [spot]):
                    return found
        return None

    return tuple(extend([0]) or range(count))


def pack_kernel(caps, routes_in, probs_in, old_in, new_in, tokens, first, second, slot_rows, *scratch):
    routes, probs, old_place, new_place, sems = scratch
    core = lax.axis_index("tensor")
    width = tokens.shape[2]
    token_count = routes.shape[2]
    experts, slots = old_place.shape[0], new_place.shape[0]
    lanes = first.shape[1] - width
    pairs = (
        (old_in, old_place),
        (new_in, new_place),
        (routes_in, routes),
        (probs_in, probs),
        (tokens.at[core], first.at[:, :width]),
        (tokens.at[1 - core], second.at[:, :width]),
    )
    copies = [pltpu.make_async_copy(src, dst, sems.at[i]) for i, (src, dst) in enumerate(pairs)]
    for copy in copies:
        copy.start()
    for copy in copies[:4]:
        copy.wait()
    token = lax.broadcasted_iota(jnp.int32, (1, token_count), 1)

    def holders_of(expert):
        return sum((new_place[s] == expert).astype(jnp.int32) for s in range(slots))

    limits = [[caps[0]] * experts, [caps[1] * holders_of(old_place[e]) for e in range(experts)]]
    for out, batch in ((first, core), (second, 1 - core)):
        highs, lows = [], []
        for e in range(experts):
            named = routes[batch] == old_place[e]
            weight = jnp.sum(jnp.where(named, probs[batch], 0.0), axis=0, keepdims=True)
            served = jnp.where(batch == 0, limits[0][e], limits[1][e])
            weight = jnp.where(token < served, weight, 0.0)
            high = weight.astype(jnp.bfloat16).astype(jnp.float32)
            highs.append(high)
            lows.append(weight - high)
        pad = jnp.zeros((lanes - 2 * experts, token_count), jnp.float32)
        out[:, width:] = jnp.concatenate(highs + lows + [pad], axis=0).T.astype(jnp.bfloat16)

    devices = lax.axis_size("expert")
    mine = slots // devices
    for j in range(mine):
        slot = lax.axis_index("expert") * mine + j
        expert = new_place[slot]
        holders = holders_of(expert)
        place = sum(
            ((new_place[s] == expert) & (s < slot)).astype(jnp.int32) for s in range(slots)
        )
        count = jnp.int32(0)
        for source in range(devices):
            start = lax.rem(place - source + devices * holders, holders)
            count += lax.div(token_count - 1 - start + holders, holders)
        slot_rows[j] = count
    for copy in copies[4:]:
        copy.wait()


def pack(caps, tokens, routes, probs, old_place, new_place):
    token_count, width = tokens.shape[1:]
    experts = old_place.shape[0]
    lanes = -(-2 * experts // LANES) * LANES
    chunk = jax.ShapeDtypeStruct((token_count, width + lanes), tokens.dtype)
    vmem, smem = pl.BlockSpec(memory_space=pltpu.VMEM), pl.BlockSpec(memory_space=pltpu.SMEM)
    mine = new_place.shape[0] // lax.axis_size("expert")
    routes, probs = routes.transpose(0, 2, 1), probs.transpose(0, 2, 1)
    return pl.pallas_call(
        functools.partial(pack_kernel, caps),
        out_shape=(chunk, chunk, jax.ShapeDtypeStruct((mine,), jnp.int32)),
        in_specs=[pl.BlockSpec(memory_space=pltpu.HBM)] * 5,
        out_specs=(vmem, vmem, smem),
        scratch_shapes=[
            pltpu.VMEM(routes.shape, routes.dtype),
            pltpu.VMEM(probs.shape, probs.dtype),
            pltpu.SMEM(old_place.shape, jnp.int32),
            pltpu.SMEM(new_place.shape, jnp.int32),
            pltpu.SemaphoreType.DMA((6,)),
        ],
        compiler_params=pltpu.CompilerParams(
            vmem_limit_bytes=VMEM_BYTES - (4 << 20)
        ),
    )(routes, probs, old_place, new_place, tokens)


def load_kernel(up, down, up_here, down_here, sems):
    copies = [
        pltpu.make_async_copy(up, up_here, sems.at[0]),
        pltpu.make_async_copy(down, down_here, sems.at[1]),
    ]
    for copy in copies:
        copy.start()
    for copy in copies:
        copy.wait()


def load(up, down):
    vmem = pl.BlockSpec(memory_space=pltpu.VMEM)
    return pl.pallas_call(
        load_kernel,
        out_shape=(
            jax.ShapeDtypeStruct(up.shape, up.dtype),
            jax.ShapeDtypeStruct(down.shape, down.dtype),
        ),
        in_specs=[pl.BlockSpec(memory_space=pltpu.HBM)] * 2,
        out_specs=(vmem, vmem),
        scratch_shapes=[pltpu.SemaphoreType.DMA((2,))],
        compiler_params=pltpu.CompilerParams(vmem_limit_bytes=VMEM_BYTES - (14 << 20)),
        cost_estimate=pl.CostEstimate(
            flops=0, bytes_accessed=4 * (up.size + down.size), transcendentals=0
        ),
    )(up, down)


def expert_kernel(chunks, width, experts, *refs):
    rows, refs = refs[:chunks], refs[chunks:]
    (up_own, up_pair, down_own, down_pair), refs = refs[:4], refs[4:]
    outs, x_buf = refs[:chunks], refs[chunks]
    slot, core = lax.axis_index("expert"), lax.axis_index("tensor")
    size = rows[0].shape[0]
    lane = lax.broadcasted_iota(jnp.int32, (size, rows[0].shape[1] - width), 1)
    mine = (lane == slot) | (lane == experts + slot)
    scales = []
    for i, row in enumerate(rows):
        x_buf[i * size : (i + 1) * size, :] = row[:, :width]
        side = row[:, width:].astype(jnp.float32)
        scales.append(jnp.sum(jnp.where(mine, side, 0.0), axis=1, keepdims=True))
    scale = jnp.concatenate(scales, axis=0)
    x = x_buf[...]
    parts = []
    for up in (up_own, up_pair):
        v = jnp.dot(x, up[...], preferred_element_type=jnp.float32)
        parts.append((v / (1.0 + jnp.exp(-v))).astype(jnp.bfloat16))
    low = jnp.where(core == 0, parts[0], parts[1])
    high = jnp.where(core == 0, parts[1], parts[0])
    hidden = jnp.concatenate([low, high], axis=1)
    half = down_own.shape[1]
    for j, down in enumerate((down_own, down_pair)):
        y = jnp.dot(hidden, down[...], preferred_element_type=jnp.float32)
        y = y.astype(jnp.bfloat16).astype(jnp.float32) * scale
        for i, out in enumerate(outs):
            out[:, j * half : (j + 1) * half] = y[i * size : (i + 1) * size].astype(out.dtype)


def expert_rows(rows, weights, width, experts, out_types):
    chunks, size = len(rows), rows[0].shape[0]
    up = weights[0]
    total = chunks * size
    vmem = pl.BlockSpec(memory_space=pltpu.VMEM)
    return pl.pallas_call(
        functools.partial(expert_kernel, chunks, width, experts),
        out_shape=[jax.ShapeDtypeStruct((size, width), t) for t in out_types],
        in_specs=[vmem] * (chunks + 4),
        out_specs=[vmem] * chunks,
        scratch_shapes=[pltpu.VMEM((total, width), jnp.bfloat16)],
        compiler_params=pltpu.CompilerParams(vmem_limit_bytes=20 << 20),
        cost_estimate=pl.CostEstimate(
            flops=2 * total * width * 4 * up.shape[1],
            bytes_accessed=8 * total * width,
            transcendentals=2 * total * up.shape[1],
        ),
    )(*rows, *weights)


def last_add_kernel(part, arrived, kept, leaving):
    half = kept.shape[1]
    kept[...] = part[:, :half] + arrived[:, :half].astype(jnp.float32)
    leaving[...] = (part[:, half:] + arrived[:, half:].astype(jnp.float32)).astype(leaving.dtype)


def last_add(part, arrived):
    size, half = part.shape[0], part.shape[1] // 2
    vmem = pl.BlockSpec(memory_space=pltpu.VMEM)
    return pl.pallas_call(
        last_add_kernel,
        out_shape=(
            jax.ShapeDtypeStruct((size, half), jnp.float32),
            jax.ShapeDtypeStruct((size, half), jnp.bfloat16),
        ),
        in_specs=[vmem, vmem],
        out_specs=(vmem, vmem),
        compiler_params=pltpu.CompilerParams(vmem_limit_bytes=4 << 20),
    )(part, arrived)


def finish_kernel(kept, from_second, second, from_first, mixed):
    core = lax.axis_index("tensor")
    half = mixed.shape[2]
    mixed[core] = (kept[...] + from_second[...].astype(jnp.float32)).astype(mixed.dtype)
    other = second[:, :half].astype(jnp.float32) + from_first[...].astype(jnp.float32)
    mixed[1 - core] = other.astype(mixed.dtype)


def finish(kept, from_second, second, from_first):
    vmem = pl.BlockSpec(memory_space=pltpu.VMEM)
    return pl.pallas_call(
        finish_kernel,
        out_shape=jax.ShapeDtypeStruct((2, *kept.shape), jnp.bfloat16),
        in_specs=[vmem] * 4,
        out_specs=vmem,
        compiler_params=pltpu.CompilerParams(vmem_limit_bytes=4 << 20),
    )(kept, from_second, second, from_first)


def by_ring(ring, tokens, routes, probs, up_weight, down_weight, old_place, new_place):
    devices = lax.axis_size("expert")
    token_count, width = tokens.shape[1], tokens.shape[2]
    experts = old_place.shape[0]
    block_rows = token_count * routes.shape[2]
    both = ("expert", "tensor")
    steps = devices // 2
    ahead = []
    for spot, here in enumerate(ring):
        there = ring[(spot + 1) % devices]
        ahead += [(2 * here, 2 * there), (2 * there + 1, 2 * here + 1)]
    back = [(b, a) for a, b in ahead]
    swap = [(0, 1), (1, 0)]
    f32, bf16 = jnp.float32, jnp.bfloat16

    caps = (
        capacity_for(block_rows, experts, token_count),
        capacity_for(block_rows, new_place.shape[0], token_count),
    )
    own_first, own_second, slot_rows = pack(caps, tokens, routes, probs, old_place, new_place)

    first, second = [own_first], [own_second]
    for step in range(1, steps + 1):
        first.append(lax.ppermute(first[-1], both, ahead))
        if step < steps:
            second.append(lax.ppermute(second[-1], both, ahead))
    up_own, down_own = up_weight[0], down_weight[0]
    up_pair = lax.ppermute(up_own, "tensor", swap)
    down_pair = lax.ppermute(down_own, "tensor", swap)
    up_here, down_here = load(up_own, down_own)
    weights = (up_here, up_pair, down_here, down_pair)

    def run(rows, out_types):
        return expert_rows(rows, weights, width, experts, out_types)

    part_first, part_second = [None] * (steps + 1), [None] * steps
    part_first[0], part_first[1], part_second[1] = run([first[0], first[1], second[1]], [f32] * 3)
    for step in range(2, steps):
        part_first[step], part_second[step] = run(
            [first[step], second[step]], [f32, bf16 if step == steps - 1 else f32]
        )
    (part_first[steps],) = run([first[steps]], [bf16])

    sum_first, sum_second = part_first[steps], part_second[steps - 1]
    for step in range(steps - 1, -1, -1):
        sum_first = lax.ppermute(sum_first, both, back)
        if step > 0:
            sum_first = (part_first[step] + sum_first.astype(f32)).astype(bf16)
        if step < steps - 1:
            sum_second = lax.ppermute(sum_second, both, back)
            if step > 0:
                sum_second = (part_second[step] + sum_second.astype(f32)).astype(bf16)
    kept, leaving = last_add(part_first[0], sum_first)
    from_second = lax.ppermute(sum_second[:, width // 2 :], "tensor", swap)
    from_first = lax.ppermute(leaving, "tensor", swap)
    return (finish(kept, from_second, sum_second, from_first), slot_rows)


def on_device(ring, tokens, routes, probs, up_weight, down_weight, old_place, new_place):
    devices = lax.axis_size("expert")
    experts = old_place.shape[0]
    arrays = (tokens, routes, probs, up_weight, down_weight, old_place, new_place)
    if (
        experts == routes.shape[2]
        and experts == devices
        and devices >= 6
        and devices % 2 == 0
        and lax.axis_size("tensor") == 2
        and tokens.shape[0] == 2
    ):
        return by_ring(ring, *arrays)
    return by_capacity(*arrays)


def solution(mesh):
    placed = (
        P(None, ("groups", "expert"), None),
        P(None, ("groups", "expert"), None),
        P(None, ("groups", "expert"), None),
        P("expert", None, "tensor"),
        P("expert", None, "tensor"),
        P("groups"),
        P("groups"),
    )
    return jax.shard_map(
        functools.partial(on_device, ring_order(mesh)),
        mesh=mesh,
        in_specs=placed,
        out_specs=(P(None, ("groups", "expert"), "tensor"), P(("groups", "expert"))),
        check_vma=False,
    )
```

```python
import functools

import jax
import jax.numpy as jnp
from jax import lax
from jax.experimental import pallas as pl
from jax.experimental.pallas import tpu as pltpu
from jax.sharding import PartitionSpec as P

REPLICAS = 4
LANES = 128
VMEM_BYTES = 67043328
PIECES = 2
SUBLANES = 16


def earlier_same(labels):
    positions = jnp.arange(labels.shape[0], dtype=jnp.int32)
    earlier = positions[None, :] < positions[:, None]
    same_label = labels[:, None] == labels[None, :]
    return jnp.sum((earlier & same_label).astype(jnp.int32), axis=1)


def holder_index(labels, holders):
    matches = labels[:, None] == holders[None, :]
    positions = jnp.arange(holders.shape[0], dtype=jnp.int32)
    return jnp.sum(matches.astype(jnp.int32) * positions[None, :], axis=1)


def replica_slots(flat_routes, new_place, source_index):
    positions = jnp.arange(new_place.shape[0], dtype=jnp.int32)
    same_slot = new_place[:, None] == new_place[None, :]
    occurrence = jnp.sum(
        (same_slot & (positions[None, :] < positions[:, None])).astype(jnp.int32), axis=1
    )
    matches = flat_routes[:, None] == new_place[None, :]
    replicas = jnp.sum(matches.astype(jnp.int32), axis=1)
    wanted = (earlier_same(flat_routes) + source_index) % replicas
    chosen = matches & (occurrence[None, :] == wanted[:, None])
    slot_ids = jnp.sum(chosen.astype(jnp.int32) * positions[None, :], axis=1)
    return (slot_ids, chosen)


def capacity_for(block_rows, targets, token_count):
    return min(token_count, max(2, (5 * block_rows + 4 * targets - 1) // (4 * targets)))


def serve_cells(tokens_mb, probs_mb, cell_ids, target_count, block, up_local, down_local):
    token_count = tokens_mb.shape[0]
    topk_count = cell_ids.shape[0] // token_count
    slots_here = up_local.shape[0]
    cells = jnp.arange(target_count * block, dtype=jnp.int32)
    placed = (cells[:, None] == cell_ids[None, :]).astype(jnp.bfloat16)
    by_token = jnp.sum(placed.reshape(target_count * block, token_count, topk_count), axis=2)
    send_rows = jnp.dot(by_token, tokens_mb, preferred_element_type=jnp.float32).astype(
        jnp.bfloat16
    )
    send_rows = send_rows.reshape(target_count, block, -1)
    received = lax.all_to_all(send_rows, "expert", split_axis=0, concat_axis=0, tiled=True)
    sources = received.shape[0] // slots_here
    grid = received.reshape(sources, slots_here, received.shape[1], received.shape[2])
    hidden = jax.nn.silu(
        jnp.einsum("nscd,sdf->nscf", grid, up_local, preferred_element_type=jnp.float32)
    ).astype(jnp.bfloat16)
    hidden = lax.all_gather(hidden, "tensor", axis=3, tiled=True)
    outputs = jnp.einsum(
        "nscf,sfd->nscd", hidden, down_local, preferred_element_type=jnp.float32
    ).astype(jnp.bfloat16)
    outputs = outputs.reshape(received.shape[0], received.shape[1], -1)
    returned = lax.all_to_all(outputs, "expert", split_axis=0, concat_axis=0, tiled=True)
    flat_back = returned.reshape(target_count * block, -1)
    picked = lax.dot_general(
        placed, flat_back, (((0,), (0,)), ((), ())), preferred_element_type=jnp.float32
    )
    weighted = picked.reshape(token_count, topk_count, -1) * probs_mb[:, :, None]
    return jnp.sum(weighted, axis=1).astype(jnp.bfloat16)


def by_capacity(tokens, routes, probs, up_weight, down_weight, old_place, new_place):
    source_index = lax.axis_index("expert")
    devices = lax.axis_size("expert")
    token_count = tokens.shape[1]
    topk_count = routes.shape[2]
    block_rows = token_count * topk_count
    expert_count = old_place.shape[0]
    slot_count = new_place.shape[0]
    early_cap = capacity_for(block_rows, expert_count, token_count)
    later_cap = capacity_for(block_rows, slot_count, token_count)
    early_routes = routes[0].reshape(-1)
    later_routes = routes[1].reshape(-1)
    early_slots = holder_index(early_routes, old_place)
    early_rank = earlier_same(early_slots)
    early_cells = jnp.where(early_rank < early_cap, early_slots * early_cap + early_rank, -1)
    later_slots, chosen = replica_slots(later_routes, new_place, source_index)
    slot_counts = lax.psum(jnp.sum(chosen.astype(jnp.int32), axis=0), "expert")
    slot_dev = slot_count // devices
    slot_rows = lax.dynamic_slice_in_dim(slot_counts, source_index * slot_dev, slot_dev, 0)
    later_rank = earlier_same(later_slots)
    later_kept = later_rank < later_cap
    early_out = serve_cells(
        tokens[0], probs[0], early_cells, expert_count, early_cap, up_weight, down_weight
    )
    homes = holder_index(later_routes, old_place)
    home_block = min(token_count, REPLICAS * later_cap)
    home_labels = jnp.where(later_kept, homes, -1)
    home_rank = earlier_same(home_labels)
    later_cells = jnp.where(later_kept, homes * home_block + home_rank, -1)
    later_out = serve_cells(
        tokens[1], probs[1], later_cells, expert_count, home_block, up_weight, down_weight
    )
    return (jnp.stack([early_out, later_out]), slot_rows)


def ring_order(mesh):
    line = mesh.devices[0, :, 0]
    count = len(line)
    if count > 16 or not all(hasattr(d, "coords") for d in line):
        return tuple(range(count))
    spots = [tuple(d.coords) for d in line]

    def near(a, b):
        return sum(abs(i - j) for i, j in zip(spots[a], spots[b])) == 1

    def extend(path):
        if len(path) == count:
            return path if near(path[-1], path[0]) else None
        for spot in range(count):
            if spot not in path and near(path[-1], spot):
                if found := extend(path + [spot]):
                    return found
        return None

    return tuple(extend([0]) or range(count))


def count_of(new_place, expert, stop):
    return sum(
        ((new_place[s] == expert) & (s < stop)).astype(jnp.int32)
        for s in range(new_place.shape[0])
    )


def pack_kernel(caps, pieces, routes_in, probs_in, old_in, new_in, tokens, *refs):
    outs, (routes, probs, old_place, new_place, sems) = refs[: 2 * pieces], refs[2 * pieces :]
    core = lax.axis_index("tensor")
    width = tokens.shape[2]
    token_count = routes.shape[2]
    experts, slots = old_place.shape[0], new_place.shape[0]
    size = token_count // pieces
    lanes = outs[0].shape[1] - width
    pairs = [(old_in, old_place), (new_in, new_place), (routes_in, routes), (probs_in, probs)]
    for i, out in enumerate(outs):
        batch = core if i < pieces else 1 - core
        rows = pl.ds(i % pieces * size, size)
        pairs.append((tokens.at[batch, rows], out.at[:, :width]))
    copies = [pltpu.make_async_copy(src, dst, sems.at[i]) for i, (src, dst) in enumerate(pairs)]
    for copy in copies:
        copy.start()
    for copy in copies[:4]:
        copy.wait()
    token = lax.broadcasted_iota(jnp.int32, (1, token_count), 1)
    limits = [caps[1] * count_of(new_place, old_place[e], slots) for e in range(experts)]
    for i, batch in enumerate((core, 1 - core)):
        highs, lows = [], []
        for e in range(experts):
            named = routes[batch] == old_place[e]
            weight = jnp.sum(jnp.where(named, probs[batch], 0.0), axis=0, keepdims=True)
            served = jnp.where(batch == 0, caps[0], limits[e])
            weight = jnp.where(token < served, weight, 0.0)
            high = weight.astype(jnp.bfloat16).astype(jnp.float32)
            highs.append(high)
            lows.append(weight - high)
        pad = jnp.zeros((lanes - 2 * experts, token_count), jnp.float32)
        side = jnp.concatenate(highs + lows + [pad], axis=0).T.astype(jnp.bfloat16)
        for j in range(pieces):
            outs[i * pieces + j][:, width:] = side[j * size : (j + 1) * size]
    for copy in copies[4:]:
        copy.wait()


def pack(caps, pieces, tokens, routes, probs, old_place, new_place):
    token_count, width = tokens.shape[1:]
    experts = old_place.shape[0]
    lanes = -(-2 * experts // LANES) * LANES
    chunk = jax.ShapeDtypeStruct((token_count // pieces, width + lanes), tokens.dtype)
    routes, probs = routes.transpose(0, 2, 1), probs.transpose(0, 2, 1)
    return pl.pallas_call(
        functools.partial(pack_kernel, caps, pieces),
        out_shape=[chunk] * (2 * pieces),
        in_specs=[pl.BlockSpec(memory_space=pltpu.HBM)] * 5,
        out_specs=[pl.BlockSpec(memory_space=pltpu.VMEM)] * (2 * pieces),
        scratch_shapes=[
            pltpu.VMEM(routes.shape, routes.dtype),
            pltpu.VMEM(probs.shape, probs.dtype),
            pltpu.SMEM(old_place.shape, jnp.int32),
            pltpu.SMEM(new_place.shape, jnp.int32),
            pltpu.SemaphoreType.DMA((4 + 2 * pieces,)),
        ],
        compiler_params=pltpu.CompilerParams(vmem_limit_bytes=VMEM_BYTES - (4 << 20)),
    )(routes, probs, old_place, new_place, tokens)


def load_kernel(devices, token_count, new_place, up, down, up_here, down_here, slot_rows, sems):
    copies = [
        pltpu.make_async_copy(up, up_here, sems.at[0]),
        pltpu.make_async_copy(down, down_here, sems.at[1]),
    ]
    for copy in copies:
        copy.start()
    mine = slot_rows.shape[0]
    for j in range(mine):
        slot = lax.axis_index("expert") * mine + j
        expert = new_place[slot]
        holders = count_of(new_place, expert, new_place.shape[0])
        place = count_of(new_place, expert, slot)
        count = jnp.int32(0)
        for source in range(devices):
            start = lax.rem(place - source + devices * holders, holders)
            count += lax.div(token_count - 1 - start + holders, holders)
        slot_rows[j] = count
    for copy in copies:
        copy.wait()


def load(up, down, new_place, devices, token_count):
    vmem, smem = pl.BlockSpec(memory_space=pltpu.VMEM), pl.BlockSpec(memory_space=pltpu.SMEM)
    hbm = pl.BlockSpec(memory_space=pltpu.HBM)
    return pl.pallas_call(
        functools.partial(load_kernel, devices, token_count),
        out_shape=(
            jax.ShapeDtypeStruct(up.shape, up.dtype),
            jax.ShapeDtypeStruct(down.shape, down.dtype),
            jax.ShapeDtypeStruct((new_place.shape[0] // devices,), jnp.int32),
        ),
        in_specs=[smem, hbm, hbm],
        out_specs=(vmem, vmem, smem),
        scratch_shapes=[pltpu.SemaphoreType.DMA((2,))],
        compiler_params=pltpu.CompilerParams(vmem_limit_bytes=VMEM_BYTES - (14 << 20)),
        cost_estimate=pl.CostEstimate(
            flops=0, bytes_accessed=4 * (up.size + down.size), transcendentals=0
        ),
    )(new_place, up, down)


def expert_kernel(chunks, width, experts, *refs):
    rows, refs = refs[:chunks], refs[chunks:]
    (up_own, up_pair, down_own, down_pair), refs = refs[:4], refs[4:]
    outs, split, x_buf = refs[:chunks], refs[chunks:-1], refs[-1]
    slot, core = lax.axis_index("expert"), lax.axis_index("tensor")
    size = rows[0].shape[0]
    lane = lax.broadcasted_iota(jnp.int32, (size, rows[0].shape[1] - width), 1)
    mine = (lane == slot) | (lane == experts + slot)
    scales = []
    for i, row in enumerate(rows):
        x_buf[i * size : (i + 1) * size, :] = row[:, :width]
        side = row[:, width:].astype(jnp.float32)
        scales.append(jnp.sum(jnp.where(mine, side, 0.0), axis=1, keepdims=True))
    scale = jnp.concatenate(scales, axis=0)
    x = x_buf[...]
    parts = []
    for up in (up_own, up_pair):
        v = jnp.dot(x, up[...], preferred_element_type=jnp.float32)
        parts.append((v / (1.0 + jnp.exp(-v))).astype(jnp.bfloat16))
    low = jnp.where(core == 0, parts[0], parts[1])
    high = jnp.where(core == 0, parts[1], parts[0])
    hidden = jnp.concatenate([low, high], axis=1)
    half = down_own.shape[1]
    for j, down in enumerate((down_own, down_pair)):
        y = jnp.dot(hidden, down[...], preferred_element_type=jnp.float32)
        y = y.astype(jnp.bfloat16).astype(jnp.float32) * scale
        for i, out in enumerate(outs):
            rows_of = y[i * size : (i + 1) * size]
            if i < len(split):
                out = (out, split[i])[j]
                out[...] = rows_of.astype(out.dtype)
            else:
                out[:, j * half : (j + 1) * half] = rows_of.astype(out.dtype)


def expert_rows(rows, weights, width, experts, out_types, splits=0):
    chunks, size = len(rows), rows[0].shape[0]
    up = weights[0]
    total = chunks * size
    vmem = pl.BlockSpec(memory_space=pltpu.VMEM)
    return pl.pallas_call(
        functools.partial(expert_kernel, chunks, width, experts),
        out_shape=[
            jax.ShapeDtypeStruct((size, width // 2 if i < splits else width), t)
            for i, t in enumerate(out_types)
        ]
        + [jax.ShapeDtypeStruct((size, width // 2), jnp.bfloat16)] * splits,
        in_specs=[vmem] * (chunks + 4),
        out_specs=[vmem] * (chunks + splits),
        scratch_shapes=[pltpu.VMEM((total, width), jnp.bfloat16)],
        compiler_params=pltpu.CompilerParams(vmem_limit_bytes=20 << 20),
        cost_estimate=pl.CostEstimate(
            flops=2 * total * width * 4 * up.shape[1],
            bytes_accessed=8 * total * width,
            transcendentals=2 * total * up.shape[1],
        ),
    )(*rows, *weights)


def split_add_kernel(part, arrived, own, pair):
    half = own.shape[1]
    own[...] = (part[:, :half] + arrived[:, :half].astype(jnp.float32)).astype(own.dtype)
    pair[...] = (part[:, half:] + arrived[:, half:].astype(jnp.float32)).astype(pair.dtype)


def split_add(part, arrived):
    size, half = part.shape[0], part.shape[1] // 2
    vmem = pl.BlockSpec(memory_space=pltpu.VMEM)
    return pl.pallas_call(
        split_add_kernel,
        out_shape=[jax.ShapeDtypeStruct((size, half), jnp.bfloat16)] * 2,
        in_specs=[vmem, vmem],
        out_specs=[vmem, vmem],
        compiler_params=pltpu.CompilerParams(vmem_limit_bytes=4 << 20),
    )(part, arrived)


def finish_kernel(pieces, *refs):
    own, arrived, second_pair, second, crossed, own_pair = (
        refs[i * pieces : (i + 1) * pieces] for i in range(6)
    )
    mixed = refs[-1]
    core = lax.axis_index("tensor")
    half = mixed.shape[2]
    size = own[0].shape[0]
    f32 = jnp.float32
    for i in range(pieces):
        rows = slice(i * size, (i + 1) * size)
        total = own[i][...] + arrived[i][...].astype(f32) + second_pair[i][...].astype(f32)
        mixed[core, rows] = total.astype(mixed.dtype)
        total = second[i][:, :half].astype(f32) + crossed[i][...].astype(f32)
        mixed[1 - core, rows] = (total + own_pair[i][...].astype(f32)).astype(mixed.dtype)


def finish(pieces, *groups):
    size, half = groups[0][0].shape
    vmem = pl.BlockSpec(memory_space=pltpu.VMEM)
    return pl.pallas_call(
        functools.partial(finish_kernel, pieces),
        out_shape=jax.ShapeDtypeStruct((2, pieces * size, half), jnp.bfloat16),
        in_specs=[vmem] * (6 * pieces),
        out_specs=vmem,
        compiler_params=pltpu.CompilerParams(vmem_limit_bytes=4 << 20),
    )(*sum((list(g) for g in groups), []))


def by_ring(ring, tokens, routes, probs, up_weight, down_weight, old_place, new_place):
    devices = lax.axis_size("expert")
    token_count, width = tokens.shape[1], tokens.shape[2]
    experts = old_place.shape[0]
    block_rows = token_count * routes.shape[2]
    both = ("expert", "tensor")
    steps = devices // 2
    ahead = []
    for spot, here in enumerate(ring):
        there = ring[(spot + 1) % devices]
        ahead += [(2 * here, 2 * there), (2 * there + 1, 2 * here + 1)]
    back = [(b, a) for a, b in ahead]
    across = [(b, a ^ 1) for a, b in ahead]
    swap = [(0, 1), (1, 0)]
    f32, bf16 = jnp.float32, jnp.bfloat16
    half, pieces = width // 2, PIECES if token_count % (PIECES * SUBLANES) == 0 else 1
    each = range(pieces)

    caps = (
        capacity_for(block_rows, experts, token_count),
        capacity_for(block_rows, new_place.shape[0], token_count),
    )
    packed = pack(caps, pieces, tokens, routes, probs, old_place, new_place)
    first, second = [packed[:pieces]], [packed[pieces:]]
    for step in range(1, steps + 1):
        first.append([lax.ppermute(first[-1][i], both, ahead) for i in each])
        if step < steps:
            second.append([lax.ppermute(second[-1][i], both, ahead) for i in each])
    up_own, down_own = up_weight[0], down_weight[0]
    up_pair = lax.ppermute(up_own, "tensor", swap)
    down_pair = lax.ppermute(down_own, "tensor", swap)
    up_here, down_here, slot_rows = load(up_own, down_own, new_place, devices, token_count)
    weights = (up_here, up_pair, down_here, down_pair)

    def run(rows, out_types, splits=0):
        return expert_rows(rows, weights, width, experts, out_types, splits)

    part_first, part_second = [None] * (steps + 1), [None] * steps
    made = run([*first[0], *first[1], *second[1]], [f32] * (3 * pieces), pieces)
    own, part_first[1], part_second[1], leaving = (
        made[i * pieces : (i + 1) * pieces] for i in range(4)
    )
    for step in range(2, steps):
        made = run(
            [*first[step], *second[step]],
            [f32] * pieces + [bf16 if step == steps - 1 else f32] * pieces,
        )
        part_first[step], part_second[step] = made[:pieces], made[pieces:]
    sum_first = run(first[steps], [bf16] * pieces)
    sum_second = part_second[steps - 1]
    own_pair = [lax.ppermute(leaving[i], "tensor", swap) for i in each]

    for step in range(steps - 2, -1, -1):
        sum_second = [lax.ppermute(sum_second[i], both, back) for i in each]
        if step > 0:
            sum_second = [
                (part + arrived.astype(f32)).astype(bf16)
                for part, arrived in zip(part_second[step], sum_second)
            ]
    second_pair = [lax.ppermute(sum_second[i][:, half:], "tensor", swap) for i in each]
    for step in range(steps - 1, 1, -1):
        sum_first = [lax.ppermute(sum_first[i], both, back) for i in each]
        sum_first = [
            (part + arrived.astype(f32)).astype(bf16)
            for part, arrived in zip(part_first[step], sum_first)
        ]
    arrived, crossed = [], []
    for i in each:
        last = lax.ppermute(sum_first[i], both, back)
        stays, crosses = split_add(part_first[1][i], last)
        arrived.append(lax.ppermute(stays, both, back))
        crossed.append(lax.ppermute(crosses, both, across))
    mixed = finish(pieces, own, arrived, second_pair, sum_second, crossed, own_pair)
    return (mixed, slot_rows)


def on_device(ring, tokens, routes, probs, up_weight, down_weight, old_place, new_place):
    devices = lax.axis_size("expert")
    experts = old_place.shape[0]
    arrays = (tokens, routes, probs, up_weight, down_weight, old_place, new_place)
    if (
        experts == routes.shape[2]
        and experts == devices
        and devices >= 6
        and devices % 2 == 0
        and lax.axis_size("tensor") == 2
        and tokens.shape[0] == 2
    ):
        return by_ring(ring, *arrays)
    return by_capacity(*arrays)


def solution(mesh):
    placed = (
        P(None, ("groups", "expert"), None),
        P(None, ("groups", "expert"), None),
        P(None, ("groups", "expert"), None),
        P("expert", None, "tensor"),
        P("expert", None, "tensor"),
        P("groups"),
        P("groups"),
    )
    return jax.shard_map(
        functools.partial(on_device, ring_order(mesh)),
        mesh=mesh,
        in_specs=placed,
        out_specs=(P(None, ("groups", "expert"), "tensor"), P(("groups", "expert"))),
        check_vma=False,
    )
```

```python
import functools

import jax
import jax.numpy as jnp
from jax import lax
from jax.experimental import pallas as pl
from jax.experimental.pallas import tpu as pltpu
from jax.sharding import PartitionSpec as P

REPLICAS = 4
LANES = 128
VMEM_BYTES = 67043328
PIECES = 2
SUBLANES = 16


def earlier_same(labels):
    positions = jnp.arange(labels.shape[0], dtype=jnp.int32)
    earlier = positions[None, :] < positions[:, None]
    same_label = labels[:, None] == labels[None, :]
    return jnp.sum((earlier & same_label).astype(jnp.int32), axis=1)


def holder_index(labels, holders):
    matches = labels[:, None] == holders[None, :]
    positions = jnp.arange(holders.shape[0], dtype=jnp.int32)
    return jnp.sum(matches.astype(jnp.int32) * positions[None, :], axis=1)


def replica_slots(flat_routes, new_place, source_index):
    positions = jnp.arange(new_place.shape[0], dtype=jnp.int32)
    same_slot = new_place[:, None] == new_place[None, :]
    occurrence = jnp.sum(
        (same_slot & (positions[None, :] < positions[:, None])).astype(jnp.int32), axis=1
    )
    matches = flat_routes[:, None] == new_place[None, :]
    replicas = jnp.sum(matches.astype(jnp.int32), axis=1)
    wanted = (earlier_same(flat_routes) + source_index) % replicas
    chosen = matches & (occurrence[None, :] == wanted[:, None])
    slot_ids = jnp.sum(chosen.astype(jnp.int32) * positions[None, :], axis=1)
    return (slot_ids, chosen)


def capacity_for(block_rows, targets, token_count):
    return min(token_count, max(2, (5 * block_rows + 4 * targets - 1) // (4 * targets)))


def serve_cells(tokens_mb, probs_mb, cell_ids, target_count, block, up_local, down_local):
    token_count = tokens_mb.shape[0]
    topk_count = cell_ids.shape[0] // token_count
    slots_here = up_local.shape[0]
    cells = jnp.arange(target_count * block, dtype=jnp.int32)
    placed = (cells[:, None] == cell_ids[None, :]).astype(jnp.bfloat16)
    by_token = jnp.sum(placed.reshape(target_count * block, token_count, topk_count), axis=2)
    send_rows = jnp.dot(by_token, tokens_mb, preferred_element_type=jnp.float32).astype(
        jnp.bfloat16
    )
    send_rows = send_rows.reshape(target_count, block, -1)
    received = lax.all_to_all(send_rows, "expert", split_axis=0, concat_axis=0, tiled=True)
    sources = received.shape[0] // slots_here
    grid = received.reshape(sources, slots_here, received.shape[1], received.shape[2])
    hidden = jax.nn.silu(
        jnp.einsum("nscd,sdf->nscf", grid, up_local, preferred_element_type=jnp.float32)
    ).astype(jnp.bfloat16)
    hidden = lax.all_gather(hidden, "tensor", axis=3, tiled=True)
    outputs = jnp.einsum(
        "nscf,sfd->nscd", hidden, down_local, preferred_element_type=jnp.float32
    ).astype(jnp.bfloat16)
    outputs = outputs.reshape(received.shape[0], received.shape[1], -1)
    returned = lax.all_to_all(outputs, "expert", split_axis=0, concat_axis=0, tiled=True)
    flat_back = returned.reshape(target_count * block, -1)
    picked = lax.dot_general(
        placed, flat_back, (((0,), (0,)), ((), ())), preferred_element_type=jnp.float32
    )
    weighted = picked.reshape(token_count, topk_count, -1) * probs_mb[:, :, None]
    return jnp.sum(weighted, axis=1).astype(jnp.bfloat16)


def by_capacity(tokens, routes, probs, up_weight, down_weight, old_place, new_place):
    source_index = lax.axis_index("expert")
    devices = lax.axis_size("expert")
    token_count = tokens.shape[1]
    topk_count = routes.shape[2]
    block_rows = token_count * topk_count
    expert_count = old_place.shape[0]
    slot_count = new_place.shape[0]
    early_cap = capacity_for(block_rows, expert_count, token_count)
    later_cap = capacity_for(block_rows, slot_count, token_count)
    early_routes = routes[0].reshape(-1)
    later_routes = routes[1].reshape(-1)
    early_slots = holder_index(early_routes, old_place)
    early_rank = earlier_same(early_slots)
    early_cells = jnp.where(early_rank < early_cap, early_slots * early_cap + early_rank, -1)
    later_slots, chosen = replica_slots(later_routes, new_place, source_index)
    slot_counts = lax.psum(jnp.sum(chosen.astype(jnp.int32), axis=0), "expert")
    slot_dev = slot_count // devices
    slot_rows = lax.dynamic_slice_in_dim(slot_counts, source_index * slot_dev, slot_dev, 0)
    later_rank = earlier_same(later_slots)
    later_kept = later_rank < later_cap
    early_out = serve_cells(
        tokens[0], probs[0], early_cells, expert_count, early_cap, up_weight, down_weight
    )
    homes = holder_index(later_routes, old_place)
    home_block = min(token_count, REPLICAS * later_cap)
    home_labels = jnp.where(later_kept, homes, -1)
    home_rank = earlier_same(home_labels)
    later_cells = jnp.where(later_kept, homes * home_block + home_rank, -1)
    later_out = serve_cells(
        tokens[1], probs[1], later_cells, expert_count, home_block, up_weight, down_weight
    )
    return (jnp.stack([early_out, later_out]), slot_rows)


def ring_order(mesh):
    line = mesh.devices[0, :, 0]
    count = len(line)
    if count > 16 or not all(hasattr(d, "coords") for d in line):
        return tuple(range(count))
    spots = [tuple(d.coords) for d in line]

    def near(a, b):
        return sum(abs(i - j) for i, j in zip(spots[a], spots[b])) == 1

    def extend(path):
        if len(path) == count:
            return path if near(path[-1], path[0]) else None
        for spot in range(count):
            if spot not in path and near(path[-1], spot):
                if found := extend(path + [spot]):
                    return found
        return None

    return tuple(extend([0]) or range(count))


def count_of(new_place, expert, stop):
    return sum(
        ((new_place[s] == expert) & (s < stop)).astype(jnp.int32)
        for s in range(new_place.shape[0])
    )


def pack_kernel(caps, routes_in, probs_in, old_in, new_in, tokens, *refs):
    first, second, slot_rows, routes, probs, old_place, new_place, sems = refs
    core, devices = lax.axis_index("tensor"), lax.axis_size("expert")
    width = tokens.shape[2]
    token_count = routes.shape[2]
    experts, slots = old_place.shape[0], new_place.shape[0]
    lanes = first.shape[1] - width
    pairs = (
        (old_in, old_place),
        (new_in, new_place),
        (routes_in, routes),
        (probs_in, probs),
        (tokens.at[core], first.at[:, :width]),
        (tokens.at[1 - core], second.at[:, :width]),
    )
    copies = [pltpu.make_async_copy(src, dst, sems.at[i]) for i, (src, dst) in enumerate(pairs)]
    for copy in copies:
        copy.start()
    for copy in copies[:4]:
        copy.wait()
    token = lax.broadcasted_iota(jnp.int32, (1, token_count), 1)
    limits = [caps[1] * count_of(new_place, old_place[e], slots) for e in range(experts)]
    for out, batch in ((first, core), (second, 1 - core)):
        highs, lows = [], []
        for e in range(experts):
            named = routes[batch] == old_place[e]
            weight = jnp.sum(jnp.where(named, probs[batch], 0.0), axis=0, keepdims=True)
            served = jnp.where(batch == 0, caps[0], limits[e])
            weight = jnp.where(token < served, weight, 0.0)
            high = weight.astype(jnp.bfloat16).astype(jnp.float32)
            highs.append(high)
            lows.append(weight - high)
        pad = jnp.zeros((lanes - 2 * experts, token_count), jnp.float32)
        out[:, width:] = jnp.concatenate(highs + lows + [pad], axis=0).T.astype(jnp.bfloat16)
    mine = slot_rows.shape[0]
    for j in range(mine):
        slot = lax.axis_index("expert") * mine + j
        expert = new_place[slot]
        holders = count_of(new_place, expert, slots)
        place = count_of(new_place, expert, slot)
        count = jnp.int32(0)
        for source in range(devices):
            start = lax.rem(place - source + devices * holders, holders)
            count += lax.div(token_count - 1 - start + holders, holders)
        slot_rows[j] = count
    for copy in copies[4:]:
        copy.wait()


def pack(caps, tokens, routes, probs, old_place, new_place):
    token_count, width = tokens.shape[1:]
    experts = old_place.shape[0]
    lanes = -(-2 * experts // LANES) * LANES
    chunk = jax.ShapeDtypeStruct((token_count, width + lanes), tokens.dtype)
    routes, probs = routes.transpose(0, 2, 1), probs.transpose(0, 2, 1)
    mine = new_place.shape[0] // lax.axis_size("expert")
    vmem, smem = pl.BlockSpec(memory_space=pltpu.VMEM), pl.BlockSpec(memory_space=pltpu.SMEM)
    return pl.pallas_call(
        functools.partial(pack_kernel, caps),
        out_shape=(chunk, chunk, jax.ShapeDtypeStruct((mine,), jnp.int32)),
        in_specs=[pl.BlockSpec(memory_space=pltpu.HBM)] * 5,
        out_specs=(vmem, vmem, smem),
        scratch_shapes=[
            pltpu.VMEM(routes.shape, routes.dtype),
            pltpu.VMEM(probs.shape, probs.dtype),
            pltpu.SMEM(old_place.shape, jnp.int32),
            pltpu.SMEM(new_place.shape, jnp.int32),
            pltpu.SemaphoreType.DMA((6,)),
        ],
        compiler_params=pltpu.CompilerParams(vmem_limit_bytes=VMEM_BYTES - (4 << 20)),
    )(routes, probs, old_place, new_place, tokens)


def load_kernel(up, down, up_here, down_here, sems):
    copies = [
        pltpu.make_async_copy(up, up_here, sems.at[0]),
        pltpu.make_async_copy(down, down_here, sems.at[1]),
    ]
    for copy in copies:
        copy.start()
    for copy in copies:
        copy.wait()


def load(up, down):
    vmem = pl.BlockSpec(memory_space=pltpu.VMEM)
    return pl.pallas_call(
        load_kernel,
        out_shape=(
            jax.ShapeDtypeStruct(up.shape, up.dtype),
            jax.ShapeDtypeStruct(down.shape, down.dtype),
        ),
        in_specs=[pl.BlockSpec(memory_space=pltpu.HBM)] * 2,
        out_specs=(vmem, vmem),
        scratch_shapes=[pltpu.SemaphoreType.DMA((2,))],
        compiler_params=pltpu.CompilerParams(vmem_limit_bytes=VMEM_BYTES - (14 << 20)),
        cost_estimate=pl.CostEstimate(
            flops=0, bytes_accessed=4 * (up.size + down.size), transcendentals=0
        ),
    )(up, down)


def expert_kernel(outlets, width, experts, *refs):
    chunks = len(outlets)
    rows, refs = refs[:chunks], refs[chunks:]
    (up_own, up_pair, down_own, down_pair), refs = refs[:4], refs[4:]
    outs, x_buf = list(refs[:-1]), refs[-1]
    slot, core = lax.axis_index("expert"), lax.axis_index("tensor")
    size = rows[0].shape[0]
    lane = lax.broadcasted_iota(jnp.int32, (size, rows[0].shape[1] - width), 1)
    mine = (lane == slot) | (lane == experts + slot)
    scales = []
    for i, row in enumerate(rows):
        x_buf[i * size : (i + 1) * size, :] = row[:, :width]
        side = row[:, width:].astype(jnp.float32)
        scales.append(jnp.sum(jnp.where(mine, side, 0.0), axis=1, keepdims=True))
    scale = jnp.concatenate(scales, axis=0)
    x = x_buf[...]
    parts = []
    for up in (up_own, up_pair):
        v = jnp.dot(x, up[...], preferred_element_type=jnp.float32)
        parts.append((v / (1.0 + jnp.exp(-v))).astype(jnp.bfloat16))
    low = jnp.where(core == 0, parts[0], parts[1])
    high = jnp.where(core == 0, parts[1], parts[0])
    hidden = jnp.concatenate([low, high], axis=1)
    half = down_own.shape[1]
    groups = []
    for kind, _ in outlets:
        groups.append([outs.pop(0) for _ in range(2 if kind == "halves" else kind)])
    for j, down in enumerate((down_own, down_pair)):
        y = jnp.dot(hidden, down[...], preferred_element_type=jnp.float32)
        y = y.astype(jnp.bfloat16).astype(jnp.float32) * scale
        for i, (kind, _) in enumerate(outlets):
            made = y[i * size : (i + 1) * size]
            if kind == "halves":
                groups[i][j][...] = made.astype(groups[i][j].dtype)
                continue
            step = size // kind
            for n, out in enumerate(groups[i]):
                piece = made[n * step : (n + 1) * step]
                out[:, j * half : (j + 1) * half] = piece.astype(out.dtype)


def expert_rows(rows, weights, width, experts, outlets):
    chunks, size = len(rows), rows[0].shape[0]
    up = weights[0]
    total = chunks * size
    vmem = pl.BlockSpec(memory_space=pltpu.VMEM)
    shapes = []
    for kind, held in outlets:
        if kind == "halves":
            shapes.append([((size, width // 2), t) for t in (jnp.float32, jnp.bfloat16)])
        else:
            shapes.append([((size // kind, width), held)] * kind)
    made = pl.pallas_call(
        functools.partial(expert_kernel, outlets, width, experts),
        out_shape=[jax.ShapeDtypeStruct(*s) for group in shapes for s in group],
        in_specs=[vmem] * (chunks + 4),
        out_specs=[vmem] * sum(len(group) for group in shapes),
        scratch_shapes=[pltpu.VMEM((total, width), jnp.bfloat16)],
        compiler_params=pltpu.CompilerParams(vmem_limit_bytes=20 << 20),
        cost_estimate=pl.CostEstimate(
            flops=2 * total * width * 4 * up.shape[1],
            bytes_accessed=8 * total * width,
            transcendentals=2 * total * up.shape[1],
        ),
    )(*rows, *weights)
    made = list(made)
    return [[made.pop(0) for _ in group] for group in shapes]


def split_add_kernel(part, arrived, own, pair):
    half = own.shape[1]
    own[...] = (part[:, :half] + arrived[:, :half].astype(jnp.float32)).astype(own.dtype)
    pair[...] = (part[:, half:] + arrived[:, half:].astype(jnp.float32)).astype(pair.dtype)


def split_add(part, arrived):
    size, half = part.shape[0], part.shape[1] // 2
    vmem = pl.BlockSpec(memory_space=pltpu.VMEM)
    return pl.pallas_call(
        split_add_kernel,
        out_shape=[jax.ShapeDtypeStruct((size, half), jnp.bfloat16)] * 2,
        in_specs=[vmem, vmem],
        out_specs=[vmem, vmem],
        compiler_params=pltpu.CompilerParams(vmem_limit_bytes=4 << 20),
    )(part, arrived)


def finish_kernel(pieces, own, own_pair, *refs):
    arrived, second_pair, second, crossed = (refs[i * pieces : (i + 1) * pieces] for i in range(4))
    mixed = refs[-1]
    core = lax.axis_index("tensor")
    half = mixed.shape[2]
    size = own.shape[0] // pieces
    f32 = jnp.float32
    for i in range(pieces):
        rows = slice(i * size, (i + 1) * size)
        total = own[rows] + arrived[i][...].astype(f32) + second_pair[i][...].astype(f32)
        mixed[core, rows] = total.astype(mixed.dtype)
        total = second[i][:, :half].astype(f32) + crossed[i][...].astype(f32)
        mixed[1 - core, rows] = (total + own_pair[rows].astype(f32)).astype(mixed.dtype)


def finish(pieces, own, own_pair, *groups):
    vmem = pl.BlockSpec(memory_space=pltpu.VMEM)
    return pl.pallas_call(
        functools.partial(finish_kernel, pieces),
        out_shape=jax.ShapeDtypeStruct((2, *own.shape), jnp.bfloat16),
        in_specs=[vmem] * (2 + 4 * pieces),
        out_specs=vmem,
        compiler_params=pltpu.CompilerParams(vmem_limit_bytes=4 << 20),
    )(own, own_pair, *sum((list(g) for g in groups), []))


def by_ring(ring, tokens, routes, probs, up_weight, down_weight, old_place, new_place):
    devices = lax.axis_size("expert")
    token_count, width = tokens.shape[1], tokens.shape[2]
    experts = old_place.shape[0]
    block_rows = token_count * routes.shape[2]
    both = ("expert", "tensor")
    steps = devices // 2
    ahead = []
    for spot, here in enumerate(ring):
        there = ring[(spot + 1) % devices]
        ahead += [(2 * here, 2 * there), (2 * there + 1, 2 * here + 1)]
    back = [(b, a) for a, b in ahead]
    across = [(b, a ^ 1) for a, b in ahead]
    swap = [(0, 1), (1, 0)]
    f32, bf16 = jnp.float32, jnp.bfloat16
    half, pieces = width // 2, PIECES if token_count % (PIECES * SUBLANES) == 0 else 1
    each = range(pieces)

    caps = (
        capacity_for(block_rows, experts, token_count),
        capacity_for(block_rows, new_place.shape[0], token_count),
    )
    own_first, own_second, slot_rows = pack(caps, tokens, routes, probs, old_place, new_place)
    first, second = [own_first], [own_second]
    for step in range(1, steps + 1):
        first.append(lax.ppermute(first[-1], both, ahead))
        if step < steps:
            second.append(lax.ppermute(second[-1], both, ahead))
    up_own, down_own = up_weight[0], down_weight[0]
    up_pair = lax.ppermute(up_own, "tensor", swap)
    down_pair = lax.ppermute(down_own, "tensor", swap)
    up_here, down_here = load(up_own, down_own)
    weights = (up_here, up_pair, down_here, down_pair)

    def run(rows, outlets):
        return expert_rows(rows, weights, width, experts, outlets)

    part_first, part_second = [None] * steps, [None] * steps
    (own, leaving), part_first[1], part_second[1] = run(
        [first[0], first[1], second[1]], [("halves", None), (pieces, f32), (pieces, f32)]
    )
    for step in range(2, steps):
        part_first[step], part_second[step] = run(
            [first[step], second[step]],
            [(pieces, f32), (pieces, bf16 if step == steps - 1 else f32)],
        )
    (sum_first,) = run([first[steps]], [(pieces, bf16)])
    sum_second = part_second[steps - 1]
    own_pair = lax.ppermute(leaving, "tensor", swap)

    for step in range(steps - 2, -1, -1):
        sum_second = [lax.ppermute(sum_second[i], both, back) for i in each]
        if step > 0:
            sum_second = [
                (part + arrived.astype(f32)).astype(bf16)
                for part, arrived in zip(part_second[step], sum_second)
            ]
    second_pair = [lax.ppermute(sum_second[i][:, half:], "tensor", swap) for i in each]
    for step in range(steps - 1, 1, -1):
        sum_first = [lax.ppermute(sum_first[i], both, back) for i in each]
        sum_first = [
            (part + arrived.astype(f32)).astype(bf16)
            for part, arrived in zip(part_first[step], sum_first)
        ]
    arrived, crossed = [], []
    for i in each:
        last = lax.ppermute(sum_first[i], both, back)
        stays, crosses = split_add(part_first[1][i], last)
        arrived.append(lax.ppermute(stays, both, back))
        crossed.append(lax.ppermute(crosses, both, across))
    mixed = finish(pieces, own, own_pair, arrived, second_pair, sum_second, crossed)
    return (mixed, slot_rows)


def on_device(ring, tokens, routes, probs, up_weight, down_weight, old_place, new_place):
    devices = lax.axis_size("expert")
    experts = old_place.shape[0]
    arrays = (tokens, routes, probs, up_weight, down_weight, old_place, new_place)
    if (
        experts == routes.shape[2]
        and experts == devices
        and devices >= 6
        and devices % 2 == 0
        and lax.axis_size("tensor") == 2
        and tokens.shape[0] == 2
    ):
        return by_ring(ring, *arrays)
    return by_capacity(*arrays)


def solution(mesh):
    placed = (
        P(None, ("groups", "expert"), None),
        P(None, ("groups", "expert"), None),
        P(None, ("groups", "expert"), None),
        P("expert", None, "tensor"),
        P("expert", None, "tensor"),
        P("groups"),
        P("groups"),
    )
    return jax.shard_map(
        functools.partial(on_device, ring_order(mesh)),
        mesh=mesh,
        in_specs=placed,
        out_specs=(P(None, ("groups", "expert"), "tensor"), P(("groups", "expert"))),
        check_vma=False,
    )
```

```python
import functools

import jax
import jax.numpy as jnp
from jax import lax
from jax.experimental import pallas as pl
from jax.experimental.pallas import tpu as pltpu
from jax.sharding import PartitionSpec as P

REPLICAS = 4
LANES = 128
VMEM_BYTES = 67043328
PIECES = 2
SUBLANES = 16


def earlier_same(labels):
    positions = jnp.arange(labels.shape[0], dtype=jnp.int32)
    earlier = positions[None, :] < positions[:, None]
    same_label = labels[:, None] == labels[None, :]
    return jnp.sum((earlier & same_label).astype(jnp.int32), axis=1)


def holder_index(labels, holders):
    matches = labels[:, None] == holders[None, :]
    positions = jnp.arange(holders.shape[0], dtype=jnp.int32)
    return jnp.sum(matches.astype(jnp.int32) * positions[None, :], axis=1)


def replica_slots(flat_routes, new_place, source_index):
    positions = jnp.arange(new_place.shape[0], dtype=jnp.int32)
    same_slot = new_place[:, None] == new_place[None, :]
    occurrence = jnp.sum(
        (same_slot & (positions[None, :] < positions[:, None])).astype(jnp.int32), axis=1
    )
    matches = flat_routes[:, None] == new_place[None, :]
    replicas = jnp.sum(matches.astype(jnp.int32), axis=1)
    wanted = (earlier_same(flat_routes) + source_index) % replicas
    chosen = matches & (occurrence[None, :] == wanted[:, None])
    slot_ids = jnp.sum(chosen.astype(jnp.int32) * positions[None, :], axis=1)
    return (slot_ids, chosen)


def capacity_for(block_rows, targets, token_count):
    return min(token_count, max(2, (5 * block_rows + 4 * targets - 1) // (4 * targets)))


def serve_cells(tokens_mb, probs_mb, cell_ids, target_count, block, up_local, down_local):
    token_count = tokens_mb.shape[0]
    topk_count = cell_ids.shape[0] // token_count
    slots_here = up_local.shape[0]
    cells = jnp.arange(target_count * block, dtype=jnp.int32)
    placed = (cells[:, None] == cell_ids[None, :]).astype(jnp.bfloat16)
    by_token = jnp.sum(placed.reshape(target_count * block, token_count, topk_count), axis=2)
    send_rows = jnp.dot(by_token, tokens_mb, preferred_element_type=jnp.float32).astype(
        jnp.bfloat16
    )
    send_rows = send_rows.reshape(target_count, block, -1)
    received = lax.all_to_all(send_rows, "expert", split_axis=0, concat_axis=0, tiled=True)
    sources = received.shape[0] // slots_here
    grid = received.reshape(sources, slots_here, received.shape[1], received.shape[2])
    hidden = jax.nn.silu(
        jnp.einsum("nscd,sdf->nscf", grid, up_local, preferred_element_type=jnp.float32)
    ).astype(jnp.bfloat16)
    hidden = lax.all_gather(hidden, "tensor", axis=3, tiled=True)
    outputs = jnp.einsum(
        "nscf,sfd->nscd", hidden, down_local, preferred_element_type=jnp.float32
    ).astype(jnp.bfloat16)
    outputs = outputs.reshape(received.shape[0], received.shape[1], -1)
    returned = lax.all_to_all(outputs, "expert", split_axis=0, concat_axis=0, tiled=True)
    flat_back = returned.reshape(target_count * block, -1)
    picked = lax.dot_general(
        placed, flat_back, (((0,), (0,)), ((), ())), preferred_element_type=jnp.float32
    )
    weighted = picked.reshape(token_count, topk_count, -1) * probs_mb[:, :, None]
    return jnp.sum(weighted, axis=1).astype(jnp.bfloat16)


def by_capacity(tokens, routes, probs, up_weight, down_weight, old_place, new_place):
    source_index = lax.axis_index("expert")
    devices = lax.axis_size("expert")
    token_count = tokens.shape[1]
    topk_count = routes.shape[2]
    block_rows = token_count * topk_count
    expert_count = old_place.shape[0]
    slot_count = new_place.shape[0]
    early_cap = capacity_for(block_rows, expert_count, token_count)
    later_cap = capacity_for(block_rows, slot_count, token_count)
    early_routes = routes[0].reshape(-1)
    later_routes = routes[1].reshape(-1)
    early_slots = holder_index(early_routes, old_place)
    early_rank = earlier_same(early_slots)
    early_cells = jnp.where(early_rank < early_cap, early_slots * early_cap + early_rank, -1)
    later_slots, chosen = replica_slots(later_routes, new_place, source_index)
    slot_counts = lax.psum(jnp.sum(chosen.astype(jnp.int32), axis=0), "expert")
    slot_dev = slot_count // devices
    slot_rows = lax.dynamic_slice_in_dim(slot_counts, source_index * slot_dev, slot_dev, 0)
    later_rank = earlier_same(later_slots)
    later_kept = later_rank < later_cap
    early_out = serve_cells(
        tokens[0], probs[0], early_cells, expert_count, early_cap, up_weight, down_weight
    )
    homes = holder_index(later_routes, old_place)
    home_block = min(token_count, REPLICAS * later_cap)
    home_labels = jnp.where(later_kept, homes, -1)
    home_rank = earlier_same(home_labels)
    later_cells = jnp.where(later_kept, homes * home_block + home_rank, -1)
    later_out = serve_cells(
        tokens[1], probs[1], later_cells, expert_count, home_block, up_weight, down_weight
    )
    return (jnp.stack([early_out, later_out]), slot_rows)


def ring_order(mesh):
    line = mesh.devices[0, :, 0]
    count = len(line)
    if count > 16 or not all(hasattr(d, "coords") for d in line):
        return tuple(range(count))
    spots = [tuple(d.coords) for d in line]

    def near(a, b):
        return sum(abs(i - j) for i, j in zip(spots[a], spots[b])) == 1

    def extend(path):
        if len(path) == count:
            return path if near(path[-1], path[0]) else None
        for spot in range(count):
            if spot not in path and near(path[-1], spot):
                if found := extend(path + [spot]):
                    return found
        return None

    return tuple(extend([0]) or range(count))


def count_of(new_place, expert, stop):
    return sum(
        ((new_place[s] == expert) & (s < stop)).astype(jnp.int32)
        for s in range(new_place.shape[0])
    )


def pack_kernel(caps, routes_in, probs_in, old_in, new_in, tokens, *refs):
    first, second, slot_rows, routes, probs, old_place, new_place, sems = refs
    core, devices = lax.axis_index("tensor"), lax.axis_size("expert")
    width = tokens.shape[2]
    token_count = routes.shape[2]
    experts, slots = old_place.shape[0], new_place.shape[0]
    lanes = first.shape[1] - width
    pairs = (
        (old_in, old_place),
        (new_in, new_place),
        (routes_in, routes),
        (probs_in, probs),
        (tokens.at[core], first.at[:, :width]),
        (tokens.at[1 - core], second.at[:, :width]),
    )
    copies = [pltpu.make_async_copy(src, dst, sems.at[i]) for i, (src, dst) in enumerate(pairs)]
    for copy in copies:
        copy.start()
    for copy in copies[:4]:
        copy.wait()
    token = lax.broadcasted_iota(jnp.int32, (1, token_count), 1)
    limits = [caps[1] * count_of(new_place, old_place[e], slots) for e in range(experts)]
    for out, batch in ((first, core), (second, 1 - core)):
        highs, lows = [], []
        for e in range(experts):
            named = routes[batch] == old_place[e]
            weight = jnp.sum(jnp.where(named, probs[batch], 0.0), axis=0, keepdims=True)
            served = jnp.where(batch == 0, caps[0], limits[e])
            weight = jnp.where(token < served, weight, 0.0)
            high = weight.astype(jnp.bfloat16).astype(jnp.float32)
            highs.append(high)
            lows.append(weight - high)
        pad = jnp.zeros((lanes - 2 * experts, token_count), jnp.float32)
        out[:, width:] = jnp.concatenate(highs + lows + [pad], axis=0).T.astype(jnp.bfloat16)
    mine = slot_rows.shape[0]
    for j in range(mine):
        slot = lax.axis_index("expert") * mine + j
        expert = new_place[slot]
        holders = count_of(new_place, expert, slots)
        place = count_of(new_place, expert, slot)
        count = jnp.int32(0)
        for source in range(devices):
            start = lax.rem(place - source + devices * holders, holders)
            count += lax.div(token_count - 1 - start + holders, holders)
        slot_rows[j] = count
    for copy in copies[4:]:
        copy.wait()


def pack(caps, tokens, routes, probs, old_place, new_place):
    token_count, width = tokens.shape[1:]
    experts = old_place.shape[0]
    lanes = -(-2 * experts // LANES) * LANES
    chunk = jax.ShapeDtypeStruct((token_count, width + lanes), tokens.dtype)
    routes, probs = routes.transpose(0, 2, 1), probs.transpose(0, 2, 1)
    mine = new_place.shape[0] // lax.axis_size("expert")
    vmem, smem = pl.BlockSpec(memory_space=pltpu.VMEM), pl.BlockSpec(memory_space=pltpu.SMEM)
    return pl.pallas_call(
        functools.partial(pack_kernel, caps),
        out_shape=(chunk, chunk, jax.ShapeDtypeStruct((mine,), jnp.int32)),
        in_specs=[pl.BlockSpec(memory_space=pltpu.HBM)] * 5,
        out_specs=(vmem, vmem, smem),
        scratch_shapes=[
            pltpu.VMEM(routes.shape, routes.dtype),
            pltpu.VMEM(probs.shape, probs.dtype),
            pltpu.SMEM(old_place.shape, jnp.int32),
            pltpu.SMEM(new_place.shape, jnp.int32),
            pltpu.SemaphoreType.DMA((6,)),
        ],
        compiler_params=pltpu.CompilerParams(vmem_limit_bytes=VMEM_BYTES - (4 << 20)),
    )(routes, probs, old_place, new_place, tokens)


def load_kernel(up, down, up_here, down_here, sems):
    copies = [
        pltpu.make_async_copy(up, up_here, sems.at[0]),
        pltpu.make_async_copy(down, down_here, sems.at[1]),
    ]
    for copy in copies:
        copy.start()
    for copy in copies:
        copy.wait()


def load(up, down):
    vmem = pl.BlockSpec(memory_space=pltpu.VMEM)
    return pl.pallas_call(
        load_kernel,
        out_shape=(
            jax.ShapeDtypeStruct(up.shape, up.dtype),
            jax.ShapeDtypeStruct(down.shape, down.dtype),
        ),
        in_specs=[pl.BlockSpec(memory_space=pltpu.HBM)] * 2,
        out_specs=(vmem, vmem),
        scratch_shapes=[pltpu.SemaphoreType.DMA((2,))],
        compiler_params=pltpu.CompilerParams(vmem_limit_bytes=VMEM_BYTES - (14 << 20)),
        cost_estimate=pl.CostEstimate(
            flops=0, bytes_accessed=4 * (up.size + down.size), transcendentals=0
        ),
    )(up, down)


def half_of(core, half):
    return pl.ds(pl.multiple_of(core * half, LANES), half)


def expert_kernel(outlets, width, experts, *refs):
    chunks = len(outlets)
    rows, refs = refs[:chunks], refs[chunks:]
    (up_own, up_pair, down_own, down_pair), refs = refs[:4], refs[4:]
    outs, x_buf = list(refs[:-1]), refs[-1]
    slot, core = lax.axis_index("expert"), lax.axis_index("tensor")
    size = rows[0].shape[0]
    lane = lax.broadcasted_iota(jnp.int32, (size, rows[0].shape[1] - width), 1)
    mine = (lane == slot) | (lane == experts + slot)
    scales = []
    for i, row in enumerate(rows):
        x_buf[i * size : (i + 1) * size, :] = row[:, :width]
        side = row[:, width:].astype(jnp.float32)
        scales.append(jnp.sum(jnp.where(mine, side, 0.0), axis=1, keepdims=True))
    scale = jnp.concatenate(scales, axis=0)
    x = x_buf[...]
    parts = []
    for up in (up_own, up_pair):
        v = jnp.dot(x, up[...], preferred_element_type=jnp.float32)
        parts.append((v / (1.0 + jnp.exp(-v))).astype(jnp.bfloat16))
    low = jnp.where(core == 0, parts[0], parts[1])
    high = jnp.where(core == 0, parts[1], parts[0])
    hidden = jnp.concatenate([low, high], axis=1)
    half = down_own.shape[1]
    groups = []
    for kind, _ in outlets:
        groups.append([outs.pop(0) for _ in range(2 if kind == "halves" else kind)])
    for j, down in enumerate((down_own, down_pair)):
        y = jnp.dot(hidden, down[...], preferred_element_type=jnp.float32)
        y = y.astype(jnp.bfloat16).astype(jnp.float32) * scale
        for i, (kind, _) in enumerate(outlets):
            made = y[i * size : (i + 1) * size]
            if kind == "halves":
                groups[i][j][...] = made.astype(groups[i][j].dtype)
                continue
            step = size // kind
            for n, out in enumerate(groups[i]):
                piece = made[n * step : (n + 1) * step]
                out[:, half_of(core if j == 0 else 1 - core, half)] = piece.astype(out.dtype)


def expert_rows(rows, weights, width, experts, outlets):
    chunks, size = len(rows), rows[0].shape[0]
    up = weights[0]
    total = chunks * size
    vmem = pl.BlockSpec(memory_space=pltpu.VMEM)
    shapes = []
    for kind, held in outlets:
        if kind == "halves":
            shapes.append([((size, width // 2), t) for t in (jnp.float32, jnp.bfloat16)])
        else:
            shapes.append([((size // kind, width), held)] * kind)
    made = pl.pallas_call(
        functools.partial(expert_kernel, outlets, width, experts),
        out_shape=[jax.ShapeDtypeStruct(*s) for group in shapes for s in group],
        in_specs=[vmem] * (chunks + 4),
        out_specs=[vmem] * sum(len(group) for group in shapes),
        scratch_shapes=[pltpu.VMEM((total, width), jnp.bfloat16)],
        compiler_params=pltpu.CompilerParams(vmem_limit_bytes=20 << 20),
        cost_estimate=pl.CostEstimate(
            flops=2 * total * width * 4 * up.shape[1],
            bytes_accessed=8 * total * width,
            transcendentals=2 * total * up.shape[1],
        ),
    )(*rows, *weights)
    made = list(made)
    return [[made.pop(0) for _ in group] for group in shapes]


def split_add_kernel(part, arrived, goes_on, crosses):
    core, half = lax.axis_index("tensor"), crosses.shape[1]
    for out, which in ((goes_on, 1 - core), (crosses, core)):
        columns = half_of(which, half)
        out[...] = (part[:, columns] + arrived[:, columns].astype(jnp.float32)).astype(out.dtype)


def split_add(part, arrived):
    size, half = part.shape[0], part.shape[1] // 2
    vmem = pl.BlockSpec(memory_space=pltpu.VMEM)
    return pl.pallas_call(
        split_add_kernel,
        out_shape=[jax.ShapeDtypeStruct((size, half), jnp.bfloat16)] * 2,
        in_specs=[vmem, vmem],
        out_specs=[vmem, vmem],
        compiler_params=pltpu.CompilerParams(vmem_limit_bytes=4 << 20),
    )(part, arrived)


def other_half_kernel(x, out):
    out[...] = x[:, half_of(1 - lax.axis_index("tensor"), out.shape[1])]


def other_half(x):
    vmem = pl.BlockSpec(memory_space=pltpu.VMEM)
    return pl.pallas_call(
        other_half_kernel,
        out_shape=jax.ShapeDtypeStruct((x.shape[0], x.shape[1] // 2), x.dtype),
        in_specs=[vmem],
        out_specs=vmem,
        compiler_params=pltpu.CompilerParams(vmem_limit_bytes=4 << 20),
    )(x)


def finish_kernel(pieces, own, own_pair, *refs):
    arrived, second_pair, second, crossed = (refs[i * pieces : (i + 1) * pieces] for i in range(4))
    mixed = refs[-1]
    core = lax.axis_index("tensor")
    half = mixed.shape[2]
    size = own.shape[0] // pieces
    f32 = jnp.float32
    for i in range(pieces):
        rows = slice(i * size, (i + 1) * size)
        total = own[rows] + arrived[i][...].astype(f32) + second_pair[i][...].astype(f32)
        mixed[core, rows] = total.astype(mixed.dtype)
        total = second[i][:, half_of(core, half)].astype(f32) + crossed[i][...].astype(f32)
        mixed[1 - core, rows] = (total + own_pair[rows].astype(f32)).astype(mixed.dtype)


def finish(pieces, own, own_pair, *groups):
    vmem = pl.BlockSpec(memory_space=pltpu.VMEM)
    return pl.pallas_call(
        functools.partial(finish_kernel, pieces),
        out_shape=jax.ShapeDtypeStruct((2, *own.shape), jnp.bfloat16),
        in_specs=[vmem] * (2 + 4 * pieces),
        out_specs=vmem,
        compiler_params=pltpu.CompilerParams(vmem_limit_bytes=4 << 20),
    )(own, own_pair, *sum((list(g) for g in groups), []))


def by_ring(ring, tokens, routes, probs, up_weight, down_weight, old_place, new_place):
    devices = lax.axis_size("expert")
    token_count, width = tokens.shape[1], tokens.shape[2]
    experts = old_place.shape[0]
    block_rows = token_count * routes.shape[2]
    both = ("expert", "tensor")
    steps = devices // 2
    ahead = []
    for spot, here in enumerate(ring):
        there = ring[(spot + 1) % devices]
        core, next_core = spot % 2, (spot + 1) % 2
        ahead.append((2 * here + core, 2 * there + next_core))
        ahead.append((2 * there + 1 - next_core, 2 * here + 1 - core))
    back = [(b, a) for a, b in ahead]
    across = [(b, a ^ 1) for a, b in ahead]
    swap = [(0, 1), (1, 0)]
    f32, bf16 = jnp.float32, jnp.bfloat16
    pieces = PIECES if token_count % (PIECES * SUBLANES) == 0 else 1
    each = range(pieces)

    caps = (
        capacity_for(block_rows, experts, token_count),
        capacity_for(block_rows, new_place.shape[0], token_count),
    )
    own_first, own_second, slot_rows = pack(caps, tokens, routes, probs, old_place, new_place)
    first, second = [own_first], [own_second]
    for step in range(1, steps + 1):
        first.append(lax.ppermute(first[-1], both, ahead))
        if step < steps:
            second.append(lax.ppermute(second[-1], both, ahead))
    up_own, down_own = up_weight[0], down_weight[0]
    up_pair = lax.ppermute(up_own, "tensor", swap)
    down_pair = lax.ppermute(down_own, "tensor", swap)
    up_here, down_here = load(up_own, down_own)
    weights = (up_here, up_pair, down_here, down_pair)

    def run(rows, outlets):
        return expert_rows(rows, weights, width, experts, outlets)

    part_first, part_second = [None] * steps, [None] * steps
    (own, leaving), part_first[1], part_second[1] = run(
        [first[0], first[1], second[1]], [("halves", None), (pieces, f32), (pieces, f32)]
    )
    for step in range(2, steps):
        part_first[step], part_second[step] = run(
            [first[step], second[step]],
            [(pieces, f32), (pieces, bf16 if step == steps - 1 else f32)],
        )
    (sum_first,) = run([first[steps]], [(pieces, bf16)])
    sum_second = part_second[steps - 1]
    own_pair = lax.ppermute(leaving, "tensor", swap)

    for step in range(steps - 2, -1, -1):
        sum_second = [lax.ppermute(sum_second[i], both, back) for i in each]
        if step > 0:
            sum_second = [
                (part + arrived.astype(f32)).astype(bf16)
                for part, arrived in zip(part_second[step], sum_second)
            ]
    second_pair = [lax.ppermute(other_half(sum_second[i]), "tensor", swap) for i in each]
    for step in range(steps - 1, 1, -1):
        sum_first = [lax.ppermute(sum_first[i], both, back) for i in each]
        sum_first = [
            (part + arrived.astype(f32)).astype(bf16)
            for part, arrived in zip(part_first[step], sum_first)
        ]
    arrived, crossed = [], []
    for i in each:
        last = lax.ppermute(sum_first[i], both, back)
        stays, crosses = split_add(part_first[1][i], last)
        arrived.append(lax.ppermute(stays, both, back))
        crossed.append(lax.ppermute(crosses, both, across))
    mixed = finish(pieces, own, own_pair, arrived, second_pair, sum_second, crossed)
    return (mixed, slot_rows)


def on_device(ring, tokens, routes, probs, up_weight, down_weight, old_place, new_place):
    devices = lax.axis_size("expert")
    experts = old_place.shape[0]
    arrays = (tokens, routes, probs, up_weight, down_weight, old_place, new_place)
    if (
        experts == routes.shape[2]
        and experts == devices
        and devices >= 6
        and devices % 2 == 0
        and lax.axis_size("tensor") == 2
        and tokens.shape[0] == 2
    ):
        return by_ring(ring, *arrays)
    return by_capacity(*arrays)


def solution(mesh):
    placed = (
        P(None, ("groups", "expert"), None),
        P(None, ("groups", "expert"), None),
        P(None, ("groups", "expert"), None),
        P("expert", None, "tensor"),
        P("expert", None, "tensor"),
        P("groups"),
        P("groups"),
    )
    return jax.shard_map(
        functools.partial(on_device, ring_order(mesh)),
        mesh=mesh,
        in_specs=placed,
        out_specs=(P(None, ("groups", "expert"), "tensor"), P(("groups", "expert"))),
        check_vma=False,
    )
```

```python
import functools

import jax
import jax.numpy as jnp
from jax import lax
from jax.experimental import pallas as pl
from jax.experimental.pallas import tpu as pltpu
from jax.sharding import PartitionSpec as P

REPLICAS = 4
LANES = 128
VMEM_BYTES = 67043328
PIECES = 2
AHEAD_FIRST = 2
AHEAD_SECOND = 2
SUBLANES = 16


def earlier_same(labels):
    positions = jnp.arange(labels.shape[0], dtype=jnp.int32)
    earlier = positions[None, :] < positions[:, None]
    same_label = labels[:, None] == labels[None, :]
    return jnp.sum((earlier & same_label).astype(jnp.int32), axis=1)


def holder_index(labels, holders):
    matches = labels[:, None] == holders[None, :]
    positions = jnp.arange(holders.shape[0], dtype=jnp.int32)
    return jnp.sum(matches.astype(jnp.int32) * positions[None, :], axis=1)


def replica_slots(flat_routes, new_place, source_index):
    positions = jnp.arange(new_place.shape[0], dtype=jnp.int32)
    same_slot = new_place[:, None] == new_place[None, :]
    occurrence = jnp.sum(
        (same_slot & (positions[None, :] < positions[:, None])).astype(jnp.int32), axis=1
    )
    matches = flat_routes[:, None] == new_place[None, :]
    replicas = jnp.sum(matches.astype(jnp.int32), axis=1)
    wanted = (earlier_same(flat_routes) + source_index) % replicas
    chosen = matches & (occurrence[None, :] == wanted[:, None])
    slot_ids = jnp.sum(chosen.astype(jnp.int32) * positions[None, :], axis=1)
    return (slot_ids, chosen)


def capacity_for(block_rows, targets, token_count):
    return min(token_count, max(2, (5 * block_rows + 4 * targets - 1) // (4 * targets)))


def serve_cells(tokens_mb, probs_mb, cell_ids, target_count, block, up_local, down_local):
    token_count = tokens_mb.shape[0]
    topk_count = cell_ids.shape[0] // token_count
    slots_here = up_local.shape[0]
    cells = jnp.arange(target_count * block, dtype=jnp.int32)
    placed = (cells[:, None] == cell_ids[None, :]).astype(jnp.bfloat16)
    by_token = jnp.sum(placed.reshape(target_count * block, token_count, topk_count), axis=2)
    send_rows = jnp.dot(by_token, tokens_mb, preferred_element_type=jnp.float32).astype(
        jnp.bfloat16
    )
    send_rows = send_rows.reshape(target_count, block, -1)
    received = lax.all_to_all(send_rows, "expert", split_axis=0, concat_axis=0, tiled=True)
    sources = received.shape[0] // slots_here
    grid = received.reshape(sources, slots_here, received.shape[1], received.shape[2])
    hidden = jax.nn.silu(
        jnp.einsum("nscd,sdf->nscf", grid, up_local, preferred_element_type=jnp.float32)
    ).astype(jnp.bfloat16)
    hidden = lax.all_gather(hidden, "tensor", axis=3, tiled=True)
    outputs = jnp.einsum(
        "nscf,sfd->nscd", hidden, down_local, preferred_element_type=jnp.float32
    ).astype(jnp.bfloat16)
    outputs = outputs.reshape(received.shape[0], received.shape[1], -1)
    returned = lax.all_to_all(outputs, "expert", split_axis=0, concat_axis=0, tiled=True)
    flat_back = returned.reshape(target_count * block, -1)
    picked = lax.dot_general(
        placed, flat_back, (((0,), (0,)), ((), ())), preferred_element_type=jnp.float32
    )
    weighted = picked.reshape(token_count, topk_count, -1) * probs_mb[:, :, None]
    return jnp.sum(weighted, axis=1).astype(jnp.bfloat16)


def by_capacity(tokens, routes, probs, up_weight, down_weight, old_place, new_place):
    source_index = lax.axis_index("expert")
    devices = lax.axis_size("expert")
    token_count = tokens.shape[1]
    topk_count = routes.shape[2]
    block_rows = token_count * topk_count
    expert_count = old_place.shape[0]
    slot_count = new_place.shape[0]
    early_cap = capacity_for(block_rows, expert_count, token_count)
    later_cap = capacity_for(block_rows, slot_count, token_count)
    early_routes = routes[0].reshape(-1)
    later_routes = routes[1].reshape(-1)
    early_slots = holder_index(early_routes, old_place)
    early_rank = earlier_same(early_slots)
    early_cells = jnp.where(early_rank < early_cap, early_slots * early_cap + early_rank, -1)
    later_slots, chosen = replica_slots(later_routes, new_place, source_index)
    slot_counts = lax.psum(jnp.sum(chosen.astype(jnp.int32), axis=0), "expert")
    slot_dev = slot_count // devices
    slot_rows = lax.dynamic_slice_in_dim(slot_counts, source_index * slot_dev, slot_dev, 0)
    later_rank = earlier_same(later_slots)
    later_kept = later_rank < later_cap
    early_out = serve_cells(
        tokens[0], probs[0], early_cells, expert_count, early_cap, up_weight, down_weight
    )
    homes = holder_index(later_routes, old_place)
    home_block = min(token_count, REPLICAS * later_cap)
    home_labels = jnp.where(later_kept, homes, -1)
    home_rank = earlier_same(home_labels)
    later_cells = jnp.where(later_kept, homes * home_block + home_rank, -1)
    later_out = serve_cells(
        tokens[1], probs[1], later_cells, expert_count, home_block, up_weight, down_weight
    )
    return (jnp.stack([early_out, later_out]), slot_rows)


def ring_order(mesh):
    line = mesh.devices[0, :, 0]
    count = len(line)
    if count > 16 or not all(hasattr(d, "coords") for d in line):
        return tuple(range(count))
    spots = [tuple(d.coords) for d in line]

    def near(a, b):
        return sum(abs(i - j) for i, j in zip(spots[a], spots[b])) == 1

    def extend(path):
        if len(path) == count:
            return path if near(path[-1], path[0]) else None
        for spot in range(count):
            if spot not in path and near(path[-1], spot):
                if found := extend(path + [spot]):
                    return found
        return None

    return tuple(extend([0]) or range(count))


def count_of(new_place, expert, stop):
    return sum(
        ((new_place[s] == expert) & (s < stop)).astype(jnp.int32)
        for s in range(new_place.shape[0])
    )


def pack_kernel(caps, pieces, routes_in, probs_in, old_in, new_in, tokens, *refs):
    count = sum(pieces)
    outs, (slot_rows, routes, probs, old_place, new_place, sems) = refs[:count], refs[count:]
    core, devices = lax.axis_index("tensor"), lax.axis_size("expert")
    width = tokens.shape[2]
    token_count = routes.shape[2]
    experts, slots = old_place.shape[0], new_place.shape[0]
    lanes = outs[0].shape[1] - width
    chunks = (outs[: pieces[0]], core), (outs[pieces[0] :], 1 - core)
    pairs = [
        (old_in, old_place),
        (new_in, new_place),
        (routes_in, routes),
        (probs_in, probs),
    ]
    for held, batch in chunks:
        size = token_count // len(held)
        for i, out in enumerate(held):
            pairs.append((tokens.at[batch, i * size : (i + 1) * size], out.at[:, :width]))
    copies = [pltpu.make_async_copy(src, dst, sems.at[i]) for i, (src, dst) in enumerate(pairs)]
    for copy in copies:
        copy.start()
    for copy in copies[:4]:
        copy.wait()
    token = lax.broadcasted_iota(jnp.int32, (1, token_count), 1)
    limits = [caps[1] * count_of(new_place, old_place[e], slots) for e in range(experts)]
    for held, batch in chunks:
        highs, lows = [], []
        for e in range(experts):
            named = routes[batch] == old_place[e]
            weight = jnp.sum(jnp.where(named, probs[batch], 0.0), axis=0, keepdims=True)
            served = jnp.where(batch == 0, caps[0], limits[e])
            weight = jnp.where(token < served, weight, 0.0)
            high = weight.astype(jnp.bfloat16).astype(jnp.float32)
            highs.append(high)
            lows.append(weight - high)
        pad = jnp.zeros((lanes - 2 * experts, token_count), jnp.float32)
        side = jnp.concatenate(highs + lows + [pad], axis=0).T.astype(jnp.bfloat16)
        size = token_count // len(held)
        for i, out in enumerate(held):
            out[:, width:] = side[i * size : (i + 1) * size]
    mine = slot_rows.shape[0]
    for j in range(mine):
        slot = lax.axis_index("expert") * mine + j
        expert = new_place[slot]
        holders = count_of(new_place, expert, slots)
        place = count_of(new_place, expert, slot)
        total = jnp.int32(0)
        for source in range(devices):
            start = lax.rem(place - source + devices * holders, holders)
            total += lax.div(token_count - 1 - start + holders, holders)
        slot_rows[j] = total
    for copy in copies[4:]:
        copy.wait()


def pack(caps, pieces, tokens, routes, probs, old_place, new_place):
    token_count, width = tokens.shape[1:]
    experts = old_place.shape[0]
    lanes = -(-2 * experts // LANES) * LANES
    chunks = [
        jax.ShapeDtypeStruct((token_count // parts, width + lanes), tokens.dtype)
        for parts in pieces
        for _ in range(parts)
    ]
    routes, probs = routes.transpose(0, 2, 1), probs.transpose(0, 2, 1)
    mine = new_place.shape[0] // lax.axis_size("expert")
    vmem, smem = pl.BlockSpec(memory_space=pltpu.VMEM), pl.BlockSpec(memory_space=pltpu.SMEM)
    return pl.pallas_call(
        functools.partial(pack_kernel, caps, pieces),
        out_shape=[*chunks, jax.ShapeDtypeStruct((mine,), jnp.int32)],
        in_specs=[pl.BlockSpec(memory_space=pltpu.HBM)] * 5,
        out_specs=[vmem] * len(chunks) + [smem],
        scratch_shapes=[
            pltpu.VMEM(routes.shape, routes.dtype),
            pltpu.VMEM(probs.shape, probs.dtype),
            pltpu.SMEM(old_place.shape, jnp.int32),
            pltpu.SMEM(new_place.shape, jnp.int32),
            pltpu.SemaphoreType.DMA((4 + len(chunks),)),
        ],
        compiler_params=pltpu.CompilerParams(vmem_limit_bytes=VMEM_BYTES - (4 << 20)),
    )(routes, probs, old_place, new_place, tokens)


def load_kernel(up, down, up_here, down_here, sems):
    copies = [
        pltpu.make_async_copy(up, up_here, sems.at[0]),
        pltpu.make_async_copy(down, down_here, sems.at[1]),
    ]
    for copy in copies:
        copy.start()
    for copy in copies:
        copy.wait()


def load(up, down):
    vmem = pl.BlockSpec(memory_space=pltpu.VMEM)
    return pl.pallas_call(
        load_kernel,
        out_shape=(
            jax.ShapeDtypeStruct(up.shape, up.dtype),
            jax.ShapeDtypeStruct(down.shape, down.dtype),
        ),
        in_specs=[pl.BlockSpec(memory_space=pltpu.HBM)] * 2,
        out_specs=(vmem, vmem),
        scratch_shapes=[pltpu.SemaphoreType.DMA((2,))],
        compiler_params=pltpu.CompilerParams(vmem_limit_bytes=VMEM_BYTES - (14 << 20)),
        cost_estimate=pl.CostEstimate(
            flops=0, bytes_accessed=4 * (up.size + down.size), transcendentals=0
        ),
    )(up, down)


def half_of(core, half):
    return pl.ds(pl.multiple_of(core * half, LANES), half)


def expert_kernel(count, outlets, width, experts, *refs):
    rows, refs = refs[:count], refs[count:]
    (up_own, up_pair, down_own, down_pair), refs = refs[:4], refs[4:]
    outs, x_buf = list(refs[:-1]), refs[-1]
    slot, core = lax.axis_index("expert"), lax.axis_index("tensor")
    scales, place = [], 0
    for row in rows:
        size = row.shape[0]
        lane = lax.broadcasted_iota(jnp.int32, (size, row.shape[1] - width), 1)
        mine = (lane == slot) | (lane == experts + slot)
        x_buf[place : place + size, :] = row[:, :width]
        place += size
        side = row[:, width:].astype(jnp.float32)
        scales.append(jnp.sum(jnp.where(mine, side, 0.0), axis=1, keepdims=True))
    scale = jnp.concatenate(scales, axis=0)
    x = x_buf[...]
    parts = []
    for up in (up_own, up_pair):
        v = jnp.dot(x, up[...], preferred_element_type=jnp.float32)
        parts.append((v / (1.0 + jnp.exp(-v))).astype(jnp.bfloat16))
    low = jnp.where(core == 0, parts[0], parts[1])
    high = jnp.where(core == 0, parts[1], parts[0])
    hidden = jnp.concatenate([low, high], axis=1)
    half = down_own.shape[1]
    groups = [[outs.pop(0) for _ in range(1 if held else 2)] for _, _, held in outlets]
    for j, down in enumerate((down_own, down_pair)):
        y = jnp.dot(hidden, down[...], preferred_element_type=jnp.float32)
        y = y.astype(jnp.bfloat16).astype(jnp.float32) * scale
        for (start, size, held), group in zip(outlets, groups):
            made = y[start : start + size]
            if held:
                columns = half_of(core if j == 0 else 1 - core, half)
                group[0][:, columns] = made.astype(held)
            else:
                group[j][...] = made.astype(group[j].dtype)


def expert_rows(rows, weights, width, experts, outlets):
    total = sum(row.shape[0] for row in rows)
    up = weights[0]
    vmem = pl.BlockSpec(memory_space=pltpu.VMEM)
    shapes = []
    for _, size, held in outlets:
        if held:
            shapes.append(((size, width), held))
        else:
            shapes += [((size, width // 2), t) for t in (jnp.float32, jnp.bfloat16)]
    return pl.pallas_call(
        functools.partial(expert_kernel, len(rows), outlets, width, experts),
        out_shape=[jax.ShapeDtypeStruct(*shape) for shape in shapes],
        in_specs=[vmem] * (len(rows) + 4),
        out_specs=[vmem] * len(shapes),
        scratch_shapes=[pltpu.VMEM((total, width), jnp.bfloat16)],
        compiler_params=pltpu.CompilerParams(vmem_limit_bytes=20 << 20),
        cost_estimate=pl.CostEstimate(
            flops=2 * total * width * 4 * up.shape[1],
            bytes_accessed=8 * total * width,
            transcendentals=2 * total * up.shape[1],
        ),
    )(*rows, *weights)


def split_add_kernel(part, arrived, goes_on, crosses):
    core, half = lax.axis_index("tensor"), crosses.shape[1]
    for out, which in ((goes_on, 1 - core), (crosses, core)):
        columns = half_of(which, half)
        out[...] = (part[:, columns] + arrived[:, columns].astype(jnp.float32)).astype(out.dtype)


def split_add(part, arrived):
    size, half = part.shape[0], part.shape[1] // 2
    vmem = pl.BlockSpec(memory_space=pltpu.VMEM)
    return pl.pallas_call(
        split_add_kernel,
        out_shape=[jax.ShapeDtypeStruct((size, half), jnp.bfloat16)] * 2,
        in_specs=[vmem, vmem],
        out_specs=[vmem, vmem],
        compiler_params=pltpu.CompilerParams(vmem_limit_bytes=4 << 20),
    )(part, arrived)


def other_half_kernel(x, out):
    out[...] = x[:, half_of(1 - lax.axis_index("tensor"), out.shape[1])]


def other_half(x):
    vmem = pl.BlockSpec(memory_space=pltpu.VMEM)
    return pl.pallas_call(
        other_half_kernel,
        out_shape=jax.ShapeDtypeStruct((x.shape[0], x.shape[1] // 2), x.dtype),
        in_specs=[vmem],
        out_specs=vmem,
        compiler_params=pltpu.CompilerParams(vmem_limit_bytes=4 << 20),
    )(x)


def finish_kernel(pieces, own, own_pair, *refs):
    arrived, second_pair, second, crossed = (refs[i * pieces : (i + 1) * pieces] for i in range(4))
    mixed = refs[-1]
    core = lax.axis_index("tensor")
    half = mixed.shape[2]
    size = own.shape[0] // pieces
    f32 = jnp.float32
    for i in range(pieces):
        rows = slice(i * size, (i + 1) * size)
        total = own[rows] + arrived[i][...].astype(f32) + second_pair[i][...].astype(f32)
        mixed[core, rows] = total.astype(mixed.dtype)
        total = second[i][:, half_of(core, half)].astype(f32) + crossed[i][...].astype(f32)
        mixed[1 - core, rows] = (total + own_pair[rows].astype(f32)).astype(mixed.dtype)


def finish(pieces, own, own_pair, *groups):
    vmem = pl.BlockSpec(memory_space=pltpu.VMEM)
    return pl.pallas_call(
        functools.partial(finish_kernel, pieces),
        out_shape=jax.ShapeDtypeStruct((2, *own.shape), jnp.bfloat16),
        in_specs=[vmem] * (2 + 4 * pieces),
        out_specs=vmem,
        compiler_params=pltpu.CompilerParams(vmem_limit_bytes=4 << 20),
    )(own, own_pair, *sum((list(g) for g in groups), []))


def by_ring(ring, tokens, routes, probs, up_weight, down_weight, old_place, new_place):
    devices = lax.axis_size("expert")
    token_count, width = tokens.shape[1], tokens.shape[2]
    experts = old_place.shape[0]
    block_rows = token_count * routes.shape[2]
    both = ("expert", "tensor")
    steps = devices // 2
    ahead = []
    for spot, here in enumerate(ring):
        there = ring[(spot + 1) % devices]
        core, next_core = spot % 2, (spot + 1) % 2
        ahead.append((2 * here + core, 2 * there + next_core))
        ahead.append((2 * there + 1 - next_core, 2 * here + 1 - core))
    back = [(b, a) for a, b in ahead]
    across = [(b, a ^ 1) for a, b in ahead]
    swap = [(0, 1), (1, 0)]
    f32, bf16 = jnp.float32, jnp.bfloat16
    each = range(PIECES)
    size = token_count // PIECES
    own_pieces = (AHEAD_FIRST, AHEAD_SECOND)

    caps = (
        capacity_for(block_rows, experts, token_count),
        capacity_for(block_rows, new_place.shape[0], token_count),
    )
    *packed, slot_rows = pack(caps, own_pieces, tokens, routes, probs, old_place, new_place)
    first, second = [packed[:AHEAD_FIRST]], [packed[AHEAD_FIRST:]]
    for step in range(1, steps + 1):
        first.append([lax.ppermute(x, both, ahead) for x in first[-1]])
        if step < steps:
            second.append([lax.ppermute(x, both, ahead) for x in second[-1]])
    up_own, down_own = up_weight[0], down_weight[0]
    up_pair = lax.ppermute(up_own, "tensor", swap)
    down_pair = lax.ppermute(down_own, "tensor", swap)
    up_here, down_here = load(up_own, down_own)
    weights = (up_here, up_pair, down_here, down_pair)

    def run(rows, outlets):
        return expert_rows(rows, weights, width, experts, outlets)

    def ranges(chunk, held):
        return [(chunk * token_count + i * size, size, held) for i in each]

    part_first, part_second = [None] * steps, [None] * steps
    own, leaving, *made = run(
        [*first[0], *first[1], *second[1]], [(0, token_count, None), *ranges(1, f32), *ranges(2, f32)]
    )
    part_first[1], part_second[1] = made[:PIECES], made[PIECES:]
    for step in range(2, steps):
        made = run([*first[step], *second[step]], ranges(0, f32) + ranges(1, bf16 if step == steps - 1 else f32))
        part_first[step], part_second[step] = made[:PIECES], made[PIECES:]
    sum_first = run(first[steps], ranges(0, bf16))
    sum_second = part_second[steps - 1]
    own_pair = lax.ppermute(leaving, "tensor", swap)

    for step in range(steps - 2, -1, -1):
        sum_second = [lax.ppermute(sum_second[i], both, back) for i in each]
        if step > 0:
            sum_second = [
                (part + arrived.astype(f32)).astype(bf16)
                for part, arrived in zip(part_second[step], sum_second)
            ]
    second_pair = [lax.ppermute(other_half(sum_second[i]), "tensor", swap) for i in each]
    for step in range(steps - 1, 1, -1):
        sum_first = [lax.ppermute(sum_first[i], both, back) for i in each]
        sum_first = [
            (part + arrived.astype(f32)).astype(bf16)
            for part, arrived in zip(part_first[step], sum_first)
        ]
    arrived, crossed = [], []
    for i in each:
        last = lax.ppermute(sum_first[i], both, back)
        stays, crosses = split_add(part_first[1][i], last)
        arrived.append(lax.ppermute(stays, both, back))
        crossed.append(lax.ppermute(crosses, both, across))
    mixed = finish(PIECES, own, own_pair, arrived, second_pair, sum_second, crossed)
    return (mixed, slot_rows)


def on_device(ring, tokens, routes, probs, up_weight, down_weight, old_place, new_place):
    devices = lax.axis_size("expert")
    experts = old_place.shape[0]
    arrays = (tokens, routes, probs, up_weight, down_weight, old_place, new_place)
    if (
        experts == routes.shape[2]
        and experts == devices
        and devices >= 6
        and devices % 2 == 0
        and lax.axis_size("tensor") == 2
        and tokens.shape[0] == 2
        and tokens.shape[1] % (SUBLANES * PIECES) == 0
        and tokens.shape[1] % (SUBLANES * AHEAD_FIRST) == 0
    ):
        return by_ring(ring, *arrays)
    return by_capacity(*arrays)


def solution(mesh):
    placed = (
        P(None, ("groups", "expert"), None),
        P(None, ("groups", "expert"), None),
        P(None, ("groups", "expert"), None),
        P("expert", None, "tensor"),
        P("expert", None, "tensor"),
        P("groups"),
        P("groups"),
    )
    return jax.shard_map(
        functools.partial(on_device, ring_order(mesh)),
        mesh=mesh,
        in_specs=placed,
        out_specs=(P(None, ("groups", "expert"), "tensor"), P(("groups", "expert"))),
        check_vma=False,
    )
```

```python
import functools

import jax
import jax.numpy as jnp
from jax import lax
from jax.experimental import pallas as pl
from jax.experimental.pallas import tpu as pltpu
from jax.sharding import PartitionSpec as P

REPLICAS = 4
LANES = 128
VMEM_BYTES = 67043328
PIECES = 2
SUBLANES = 16


def earlier_same(labels):
    positions = jnp.arange(labels.shape[0], dtype=jnp.int32)
    earlier = positions[None, :] < positions[:, None]
    same_label = labels[:, None] == labels[None, :]
    return jnp.sum((earlier & same_label).astype(jnp.int32), axis=1)


def holder_index(labels, holders):
    matches = labels[:, None] == holders[None, :]
    positions = jnp.arange(holders.shape[0], dtype=jnp.int32)
    return jnp.sum(matches.astype(jnp.int32) * positions[None, :], axis=1)


def replica_slots(flat_routes, new_place, source_index):
    positions = jnp.arange(new_place.shape[0], dtype=jnp.int32)
    same_slot = new_place[:, None] == new_place[None, :]
    occurrence = jnp.sum(
        (same_slot & (positions[None, :] < positions[:, None])).astype(jnp.int32), axis=1
    )
    matches = flat_routes[:, None] == new_place[None, :]
    replicas = jnp.sum(matches.astype(jnp.int32), axis=1)
    wanted = (earlier_same(flat_routes) + source_index) % replicas
    chosen = matches & (occurrence[None, :] == wanted[:, None])
    slot_ids = jnp.sum(chosen.astype(jnp.int32) * positions[None, :], axis=1)
    return (slot_ids, chosen)


def capacity_for(block_rows, targets, token_count):
    return min(token_count, max(2, (5 * block_rows + 4 * targets - 1) // (4 * targets)))


def serve_cells(tokens_mb, probs_mb, cell_ids, target_count, block, up_local, down_local):
    token_count = tokens_mb.shape[0]
    topk_count = cell_ids.shape[0] // token_count
    slots_here = up_local.shape[0]
    cells = jnp.arange(target_count * block, dtype=jnp.int32)
    placed = (cells[:, None] == cell_ids[None, :]).astype(jnp.bfloat16)
    by_token = jnp.sum(placed.reshape(target_count * block, token_count, topk_count), axis=2)
    send_rows = jnp.dot(by_token, tokens_mb, preferred_element_type=jnp.float32).astype(
        jnp.bfloat16
    )
    send_rows = send_rows.reshape(target_count, block, -1)
    received = lax.all_to_all(send_rows, "expert", split_axis=0, concat_axis=0, tiled=True)
    sources = received.shape[0] // slots_here
    grid = received.reshape(sources, slots_here, received.shape[1], received.shape[2])
    hidden = jax.nn.silu(
        jnp.einsum("nscd,sdf->nscf", grid, up_local, preferred_element_type=jnp.float32)
    ).astype(jnp.bfloat16)
    hidden = lax.all_gather(hidden, "tensor", axis=3, tiled=True)
    outputs = jnp.einsum(
        "nscf,sfd->nscd", hidden, down_local, preferred_element_type=jnp.float32
    ).astype(jnp.bfloat16)
    outputs = outputs.reshape(received.shape[0], received.shape[1], -1)
    returned = lax.all_to_all(outputs, "expert", split_axis=0, concat_axis=0, tiled=True)
    flat_back = returned.reshape(target_count * block, -1)
    picked = lax.dot_general(
        placed, flat_back, (((0,), (0,)), ((), ())), preferred_element_type=jnp.float32
    )
    weighted = picked.reshape(token_count, topk_count, -1) * probs_mb[:, :, None]
    return jnp.sum(weighted, axis=1).astype(jnp.bfloat16)


def by_capacity(tokens, routes, probs, up_weight, down_weight, old_place, new_place):
    source_index = lax.axis_index("expert")
    devices = lax.axis_size("expert")
    token_count = tokens.shape[1]
    topk_count = routes.shape[2]
    block_rows = token_count * topk_count
    expert_count = old_place.shape[0]
    slot_count = new_place.shape[0]
    early_cap = capacity_for(block_rows, expert_count, token_count)
    later_cap = capacity_for(block_rows, slot_count, token_count)
    early_routes = routes[0].reshape(-1)
    later_routes = routes[1].reshape(-1)
    early_slots = holder_index(early_routes, old_place)
    early_rank = earlier_same(early_slots)
    early_cells = jnp.where(early_rank < early_cap, early_slots * early_cap + early_rank, -1)
    later_slots, chosen = replica_slots(later_routes, new_place, source_index)
    slot_counts = lax.psum(jnp.sum(chosen.astype(jnp.int32), axis=0), "expert")
    slot_dev = slot_count // devices
    slot_rows = lax.dynamic_slice_in_dim(slot_counts, source_index * slot_dev, slot_dev, 0)
    later_rank = earlier_same(later_slots)
    later_kept = later_rank < later_cap
    early_out = serve_cells(
        tokens[0], probs[0], early_cells, expert_count, early_cap, up_weight, down_weight
    )
    homes = holder_index(later_routes, old_place)
    home_block = min(token_count, REPLICAS * later_cap)
    home_labels = jnp.where(later_kept, homes, -1)
    home_rank = earlier_same(home_labels)
    later_cells = jnp.where(later_kept, homes * home_block + home_rank, -1)
    later_out = serve_cells(
        tokens[1], probs[1], later_cells, expert_count, home_block, up_weight, down_weight
    )
    return (jnp.stack([early_out, later_out]), slot_rows)


def ring_order(mesh):
    line = mesh.devices[0, :, 0]
    count = len(line)
    if count > 16 or not all(hasattr(d, "coords") for d in line):
        return tuple(range(count))
    spots = [tuple(d.coords) for d in line]

    def near(a, b):
        return sum(abs(i - j) for i, j in zip(spots[a], spots[b])) == 1

    def extend(path):
        if len(path) == count:
            return path if near(path[-1], path[0]) else None
        for spot in range(count):
            if spot not in path and near(path[-1], spot):
                if found := extend(path + [spot]):
                    return found
        return None

    return tuple(extend([0]) or range(count))


def count_of(new_place, expert, stop):
    return sum(
        ((new_place[s] == expert) & (s < stop)).astype(jnp.int32)
        for s in range(new_place.shape[0])
    )


def side_lanes(experts):
    return -(-4 * PIECES * experts // LANES) * LANES


def pack_kernel(caps, routes_in, probs_in, old_in, new_in, tokens, *refs):
    outs, refs = refs[: 2 * PIECES], refs[2 * PIECES :]
    slot_rows, routes, probs, old_place, new_place, sems = refs
    core, devices = lax.axis_index("tensor"), lax.axis_size("expert")
    width = tokens.shape[2]
    topk_count, token_count = routes.shape[1:]
    experts, slots = old_place.shape[0], new_place.shape[0]
    size = token_count // PIECES
    pairs = [(old_in, old_place), (new_in, new_place), (routes_in, routes), (probs_in, probs)]
    for i, out in enumerate(outs):
        batch = core if i < PIECES else 1 - core
        start = i % PIECES * size
        pairs.append((tokens.at[batch, start : start + size], out.at[:, :width]))
    copies = [pltpu.make_async_copy(src, dst, sems.at[i]) for i, (src, dst) in enumerate(pairs)]
    for copy in copies:
        copy.start()
    for copy in copies[:4]:
        copy.wait()
    slot = lax.broadcasted_iota(jnp.int32, (experts, token_count), 0)
    token = lax.broadcasted_iota(jnp.int32, (experts, token_count), 1)
    held, limit = jnp.zeros_like(slot), jnp.zeros_like(slot)
    for e in range(experts):
        held = jnp.where(slot == e, old_place[e], held)
        limit = jnp.where(slot == e, caps[1] * count_of(new_place, old_place[e], slots), limit)
    kinds = []
    for batch in (core, 1 - core):
        named, chance = routes[batch], probs[batch]
        weight = jnp.zeros((experts, token_count), jnp.float32)
        for k in range(topk_count):
            weight += jnp.where(named[k : k + 1] == held, chance[k : k + 1], 0.0)
        weight = jnp.where(token < jnp.where(batch == 0, caps[0], limit), weight, 0.0)
        high = weight.astype(jnp.bfloat16).astype(jnp.float32)
        kinds += [high, weight - high]
    lanes = side_lanes(experts)
    kinds.append(jnp.zeros((lanes - 4 * experts, token_count), jnp.float32))
    turned = jnp.concatenate(kinds, axis=0).T
    side = turned[:size]
    for i in range(1, PIECES):
        side += pltpu.roll(turned[i * size : (i + 1) * size], 4 * experts * i, 1)
    outs[PIECES - 1][:, width:] = side.astype(jnp.bfloat16)
    mine = slot_rows.shape[0]
    for j in range(mine):
        new_slot = lax.axis_index("expert") * mine + j
        expert = new_place[new_slot]
        holders = count_of(new_place, expert, slots)
        place = count_of(new_place, expert, new_slot)
        total = jnp.int32(0)
        for source in range(devices):
            start = lax.rem(place - source + devices * holders, holders)
            total += lax.div(token_count - 1 - start + holders, holders)
        slot_rows[j] = total
    for copy in copies[4:]:
        copy.wait()


def pack(caps, tokens, routes, probs, old_place, new_place):
    token_count, width = tokens.shape[1:]
    experts = old_place.shape[0]
    size = token_count // PIECES
    widths = [width] * (2 * PIECES)
    widths[PIECES - 1] += side_lanes(experts)
    routes, probs = routes.transpose(0, 2, 1), probs.transpose(0, 2, 1)
    mine = new_place.shape[0] // lax.axis_size("expert")
    vmem, smem = pl.BlockSpec(memory_space=pltpu.VMEM), pl.BlockSpec(memory_space=pltpu.SMEM)
    return pl.pallas_call(
        functools.partial(pack_kernel, caps),
        out_shape=[jax.ShapeDtypeStruct((size, w), tokens.dtype) for w in widths]
        + [jax.ShapeDtypeStruct((mine,), jnp.int32)],
        in_specs=[pl.BlockSpec(memory_space=pltpu.HBM)] * 5,
        out_specs=[vmem] * len(widths) + [smem],
        scratch_shapes=[
            pltpu.VMEM(routes.shape, routes.dtype),
            pltpu.VMEM(probs.shape, probs.dtype),
            pltpu.SMEM(old_place.shape, jnp.int32),
            pltpu.SMEM(new_place.shape, jnp.int32),
            pltpu.SemaphoreType.DMA((4 + len(widths),)),
        ],
        compiler_params=pltpu.CompilerParams(vmem_limit_bytes=VMEM_BYTES - (4 << 20)),
    )(routes, probs, old_place, new_place, tokens)


def half_of(core, half):
    return pl.ds(pl.multiple_of(core * half, LANES), half)


def expert_kernel(sides, outlets, width, experts, *refs):
    count = len(sides)
    rows, refs = refs[:count], refs[count:]
    (up_own, up_pair, down_own, down_pair), refs = refs[:4], refs[4:]
    outs, x_buf = list(refs[:-1]), refs[-1]
    slot, core = lax.axis_index("expert"), lax.axis_index("tensor")
    scales, place = [], 0
    for row, (holder, offset) in zip(rows, sides):
        x_buf[place : place + row.shape[0], :] = row[:, :width]
        place += row.shape[0]
        side = rows[holder][:, width:].astype(jnp.float32)
        lane = lax.broadcasted_iota(jnp.int32, side.shape, 1) - offset - slot
        mine = (lane == 0) | (lane == experts)
        scales.append(jnp.sum(jnp.where(mine, side, 0.0), axis=1, keepdims=True))
    scale = jnp.concatenate(scales, axis=0)
    x = x_buf[...]
    parts = []
    for up in (up_own, up_pair):
        v = jnp.dot(x, up[...], preferred_element_type=jnp.float32)
        parts.append((v / (1.0 + jnp.exp(-v))).astype(jnp.bfloat16))
    low = jnp.where(core == 0, parts[0], parts[1])
    high = jnp.where(core == 0, parts[1], parts[0])
    hidden = jnp.concatenate([low, high], axis=1)
    half = down_own.shape[1]
    groups = [[outs.pop(0) for _ in range(1 if held else 2)] for _, _, held in outlets]
    for j, down in enumerate((down_own, down_pair)):
        y = jnp.dot(hidden, down[...], preferred_element_type=jnp.float32)
        y = y.astype(jnp.bfloat16).astype(jnp.float32) * scale
        for (start, size, held), group in zip(outlets, groups):
            made = y[start : start + size]
            if held:
                columns = half_of(core if j == 0 else 1 - core, half)
                group[0][:, columns] = made.astype(held)
            else:
                group[j][...] = made.astype(group[j].dtype)


def expert_rows(hops, weights, width, experts, outlets):
    rows, sides = [], []
    for pieces in hops:
        holder = len(rows) + PIECES - 1
        for i in range(len(pieces)):
            chunk, piece = divmod(i, PIECES)
            sides.append((holder, (4 * piece + 2 * chunk) * experts))
        rows += pieces
    total = sum(row.shape[0] for row in rows)
    up = weights[0]
    vmem = pl.BlockSpec(memory_space=pltpu.VMEM)
    shapes = []
    for _, size, held in outlets:
        if held:
            shapes.append(((size, width), held))
        else:
            shapes += [((size, width // 2), t) for t in (jnp.float32, jnp.bfloat16)]
    return pl.pallas_call(
        functools.partial(expert_kernel, tuple(sides), outlets, width, experts),
        out_shape=[jax.ShapeDtypeStruct(*shape) for shape in shapes],
        in_specs=[vmem] * (len(rows) + 4),
        out_specs=[vmem] * len(shapes),
        scratch_shapes=[pltpu.VMEM((total, width), jnp.bfloat16)],
        compiler_params=pltpu.CompilerParams(vmem_limit_bytes=20 << 20),
        cost_estimate=pl.CostEstimate(
            flops=2 * total * width * 4 * up.shape[1],
            bytes_accessed=8 * total * width,
            transcendentals=2 * total * up.shape[1],
        ),
    )(*rows, *weights)


def split_add_kernel(part, arrived, goes_on, crosses):
    core, half = lax.axis_index("tensor"), crosses.shape[1]
    for out, which in ((goes_on, 1 - core), (crosses, core)):
        columns = half_of(which, half)
        out[...] = (part[:, columns] + arrived[:, columns].astype(jnp.float32)).astype(out.dtype)


def split_add(part, arrived):
    size, half = part.shape[0], part.shape[1] // 2
    vmem = pl.BlockSpec(memory_space=pltpu.VMEM)
    return pl.pallas_call(
        split_add_kernel,
        out_shape=[jax.ShapeDtypeStruct((size, half), jnp.bfloat16)] * 2,
        in_specs=[vmem, vmem],
        out_specs=[vmem, vmem],
        compiler_params=pltpu.CompilerParams(vmem_limit_bytes=4 << 20),
    )(part, arrived)


def other_half_kernel(x, out):
    out[...] = x[:, half_of(1 - lax.axis_index("tensor"), out.shape[1])]


def other_half(x):
    vmem = pl.BlockSpec(memory_space=pltpu.VMEM)
    return pl.pallas_call(
        other_half_kernel,
        out_shape=jax.ShapeDtypeStruct((x.shape[0], x.shape[1] // 2), x.dtype),
        in_specs=[vmem],
        out_specs=vmem,
        compiler_params=pltpu.CompilerParams(vmem_limit_bytes=4 << 20),
    )(x)


def finish_kernel(pieces, own, own_pair, *refs):
    arrived, second_pair, second, crossed = (refs[i * pieces : (i + 1) * pieces] for i in range(4))
    mixed = refs[-1]
    core = lax.axis_index("tensor")
    half = mixed.shape[2]
    size = own.shape[0] // pieces
    f32 = jnp.float32
    for i in range(pieces):
        rows = slice(i * size, (i + 1) * size)
        total = own[rows] + arrived[i][...].astype(f32) + second_pair[i][...].astype(f32)
        mixed[core, rows] = total.astype(mixed.dtype)
        total = second[i][:, half_of(core, half)].astype(f32) + crossed[i][...].astype(f32)
        mixed[1 - core, rows] = (total + own_pair[rows].astype(f32)).astype(mixed.dtype)


def finish(pieces, own, own_pair, *groups):
    vmem = pl.BlockSpec(memory_space=pltpu.VMEM)
    return pl.pallas_call(
        functools.partial(finish_kernel, pieces),
        out_shape=jax.ShapeDtypeStruct((2, *own.shape), jnp.bfloat16),
        in_specs=[vmem] * (2 + 4 * pieces),
        out_specs=vmem,
        compiler_params=pltpu.CompilerParams(vmem_limit_bytes=4 << 20),
    )(own, own_pair, *sum((list(g) for g in groups), []))


def by_ring(ring, tokens, routes, probs, up_weight, down_weight, old_place, new_place):
    devices = lax.axis_size("expert")
    token_count, width = tokens.shape[1], tokens.shape[2]
    experts = old_place.shape[0]
    block_rows = token_count * routes.shape[2]
    both = ("expert", "tensor")
    steps = devices // 2
    ahead = []
    for spot, here in enumerate(ring):
        there = ring[(spot + 1) % devices]
        core, next_core = spot % 2, (spot + 1) % 2
        ahead.append((2 * here + core, 2 * there + next_core))
        ahead.append((2 * there + 1 - next_core, 2 * here + 1 - core))
    back = [(b, a) for a, b in ahead]
    across = [(b, a ^ 1) for a, b in ahead]
    swap = [(0, 1), (1, 0)]
    f32, bf16 = jnp.float32, jnp.bfloat16
    each = range(PIECES)
    size = token_count // PIECES

    caps = (
        capacity_for(block_rows, experts, token_count),
        capacity_for(block_rows, new_place.shape[0], token_count),
    )
    *packed, slot_rows = pack(caps, tokens, routes, probs, old_place, new_place)
    first, second = [packed[:PIECES]], [packed[PIECES:]]
    for step in range(1, steps + 1):
        first.append([lax.ppermute(first[-1][i], both, ahead) for i in each])
        if step < steps:
            second.append([lax.ppermute(second[-1][i], both, ahead) for i in each])
    up_own, down_own = up_weight[0], down_weight[0]
    up_pair = lax.ppermute(up_own, "tensor", swap)
    down_pair = lax.ppermute(down_own, "tensor", swap)
    up_here = lax.ppermute(up_pair, "tensor", swap)
    down_here = lax.ppermute(down_pair, "tensor", swap)
    weights = (up_here, up_pair, down_here, down_pair)

    def run(held, outlets):
        return expert_rows(held, weights, width, experts, outlets)

    def ranges(chunk, held):
        return [(chunk * token_count + i * size, size, held) for i in each]

    part_first, part_second = [None] * steps, [None] * steps
    own, leaving, *made = run(
        [first[0], first[1] + second[1]], [(0, token_count, None), *ranges(1, f32), *ranges(2, f32)]
    )
    part_first[1], part_second[1] = made[:PIECES], made[PIECES:]
    for step in range(2, steps):
        made = run([first[step] + second[step]], ranges(0, f32) + ranges(1, bf16 if step == steps - 1 else f32))
        part_first[step], part_second[step] = made[:PIECES], made[PIECES:]
    sum_first = run([first[steps]], ranges(0, bf16))
    sum_second = part_second[steps - 1]
    own_pair = lax.ppermute(leaving, "tensor", swap)

    for step in range(steps - 2, -1, -1):
        sum_second = [lax.ppermute(sum_second[i], both, back) for i in each]
        if step > 0:
            sum_second = [
                (part + arrived.astype(f32)).astype(bf16)
                for part, arrived in zip(part_second[step], sum_second)
            ]
    second_pair = [lax.ppermute(other_half(sum_second[i]), "tensor", swap) for i in each]
    for step in range(steps - 1, 1, -1):
        sum_first = [lax.ppermute(sum_first[i], both, back) for i in each]
        sum_first = [
            (part + arrived.astype(f32)).astype(bf16)
            for part, arrived in zip(part_first[step], sum_first)
        ]
    arrived, crossed = [], []
    for i in each:
        last = lax.ppermute(sum_first[i], both, back)
        stays, crosses = split_add(part_first[1][i], last)
        arrived.append(lax.ppermute(stays, both, back))
        crossed.append(lax.ppermute(crosses, both, across))
    mixed = finish(PIECES, own, own_pair, arrived, second_pair, sum_second, crossed)
    return (mixed, slot_rows)


def on_device(ring, tokens, routes, probs, up_weight, down_weight, old_place, new_place):
    devices = lax.axis_size("expert")
    experts = old_place.shape[0]
    arrays = (tokens, routes, probs, up_weight, down_weight, old_place, new_place)
    if (
        experts == routes.shape[2]
        and experts == devices
        and devices >= 6
        and devices % 2 == 0
        and lax.axis_size("tensor") == 2
        and tokens.shape[0] == 2
        and tokens.shape[1] % (SUBLANES * PIECES) == 0
    ):
        return by_ring(ring, *arrays)
    return by_capacity(*arrays)


def solution(mesh):
    placed = (
        P(None, ("groups", "expert"), None),
        P(None, ("groups", "expert"), None),
        P(None, ("groups", "expert"), None),
        P("expert", None, "tensor"),
        P("expert", None, "tensor"),
        P("groups"),
        P("groups"),
    )
    return jax.shard_map(
        functools.partial(on_device, ring_order(mesh)),
        mesh=mesh,
        in_specs=placed,
        out_specs=(P(None, ("groups", "expert"), "tensor"), P(("groups", "expert"))),
        check_vma=False,
    )
```

```python
import functools

import jax
import jax.numpy as jnp
from jax import lax
from jax.experimental import pallas as pl
from jax.experimental.pallas import tpu as pltpu
from jax.sharding import PartitionSpec as P

REPLICAS = 4
LANES = 128
VMEM_BYTES = 67043328
PIECES = 2
SUBLANES = 16


def earlier_same(labels):
    positions = jnp.arange(labels.shape[0], dtype=jnp.int32)
    earlier = positions[None, :] < positions[:, None]
    same_label = labels[:, None] == labels[None, :]
    return jnp.sum((earlier & same_label).astype(jnp.int32), axis=1)


def holder_index(labels, holders):
    matches = labels[:, None] == holders[None, :]
    positions = jnp.arange(holders.shape[0], dtype=jnp.int32)
    return jnp.sum(matches.astype(jnp.int32) * positions[None, :], axis=1)


def replica_slots(flat_routes, new_place, source_index):
    positions = jnp.arange(new_place.shape[0], dtype=jnp.int32)
    same_slot = new_place[:, None] == new_place[None, :]
    occurrence = jnp.sum(
        (same_slot & (positions[None, :] < positions[:, None])).astype(jnp.int32), axis=1
    )
    matches = flat_routes[:, None] == new_place[None, :]
    replicas = jnp.sum(matches.astype(jnp.int32), axis=1)
    wanted = (earlier_same(flat_routes) + source_index) % replicas
    chosen = matches & (occurrence[None, :] == wanted[:, None])
    slot_ids = jnp.sum(chosen.astype(jnp.int32) * positions[None, :], axis=1)
    return (slot_ids, chosen)


def capacity_for(block_rows, targets, token_count):
    return min(token_count, max(2, (5 * block_rows + 4 * targets - 1) // (4 * targets)))


def serve_cells(tokens_mb, probs_mb, cell_ids, target_count, block, up_local, down_local):
    token_count = tokens_mb.shape[0]
    topk_count = cell_ids.shape[0] // token_count
    slots_here = up_local.shape[0]
    cells = jnp.arange(target_count * block, dtype=jnp.int32)
    placed = (cells[:, None] == cell_ids[None, :]).astype(jnp.bfloat16)
    by_token = jnp.sum(placed.reshape(target_count * block, token_count, topk_count), axis=2)
    send_rows = jnp.dot(by_token, tokens_mb, preferred_element_type=jnp.float32).astype(
        jnp.bfloat16
    )
    send_rows = send_rows.reshape(target_count, block, -1)
    received = lax.all_to_all(send_rows, "expert", split_axis=0, concat_axis=0, tiled=True)
    sources = received.shape[0] // slots_here
    grid = received.reshape(sources, slots_here, received.shape[1], received.shape[2])
    hidden = jax.nn.silu(
        jnp.einsum("nscd,sdf->nscf", grid, up_local, preferred_element_type=jnp.float32)
    ).astype(jnp.bfloat16)
    hidden = lax.all_gather(hidden, "tensor", axis=3, tiled=True)
    outputs = jnp.einsum(
        "nscf,sfd->nscd", hidden, down_local, preferred_element_type=jnp.float32
    ).astype(jnp.bfloat16)
    outputs = outputs.reshape(received.shape[0], received.shape[1], -1)
    returned = lax.all_to_all(outputs, "expert", split_axis=0, concat_axis=0, tiled=True)
    flat_back = returned.reshape(target_count * block, -1)
    picked = lax.dot_general(
        placed, flat_back, (((0,), (0,)), ((), ())), preferred_element_type=jnp.float32
    )
    weighted = picked.reshape(token_count, topk_count, -1) * probs_mb[:, :, None]
    return jnp.sum(weighted, axis=1).astype(jnp.bfloat16)


def by_capacity(tokens, routes, probs, up_weight, down_weight, old_place, new_place):
    source_index = lax.axis_index("expert")
    devices = lax.axis_size("expert")
    token_count = tokens.shape[1]
    topk_count = routes.shape[2]
    block_rows = token_count * topk_count
    expert_count = old_place.shape[0]
    slot_count = new_place.shape[0]
    early_cap = capacity_for(block_rows, expert_count, token_count)
    later_cap = capacity_for(block_rows, slot_count, token_count)
    early_routes = routes[0].reshape(-1)
    later_routes = routes[1].reshape(-1)
    early_slots = holder_index(early_routes, old_place)
    early_rank = earlier_same(early_slots)
    early_cells = jnp.where(early_rank < early_cap, early_slots * early_cap + early_rank, -1)
    later_slots, chosen = replica_slots(later_routes, new_place, source_index)
    slot_counts = lax.psum(jnp.sum(chosen.astype(jnp.int32), axis=0), "expert")
    slot_dev = slot_count // devices
    slot_rows = lax.dynamic_slice_in_dim(slot_counts, source_index * slot_dev, slot_dev, 0)
    later_rank = earlier_same(later_slots)
    later_kept = later_rank < later_cap
    early_out = serve_cells(
        tokens[0], probs[0], early_cells, expert_count, early_cap, up_weight, down_weight
    )
    homes = holder_index(later_routes, old_place)
    home_block = min(token_count, REPLICAS * later_cap)
    home_labels = jnp.where(later_kept, homes, -1)
    home_rank = earlier_same(home_labels)
    later_cells = jnp.where(later_kept, homes * home_block + home_rank, -1)
    later_out = serve_cells(
        tokens[1], probs[1], later_cells, expert_count, home_block, up_weight, down_weight
    )
    return (jnp.stack([early_out, later_out]), slot_rows)


def ring_order(mesh):
    line = mesh.devices[0, :, 0]
    count = len(line)
    if count > 16 or not all(hasattr(d, "coords") for d in line):
        return tuple(range(count))
    spots = [tuple(d.coords) for d in line]

    def near(a, b):
        return sum(abs(i - j) for i, j in zip(spots[a], spots[b])) == 1

    def extend(path):
        if len(path) == count:
            return path if near(path[-1], path[0]) else None
        for spot in range(count):
            if spot not in path and near(path[-1], spot):
                if found := extend(path + [spot]):
                    return found
        return None

    return tuple(extend([0]) or range(count))


def count_of(new_place, expert, stop):
    return sum(
        ((new_place[s] == expert) & (s < stop)).astype(jnp.int32)
        for s in range(new_place.shape[0])
    )


def side_lanes(experts):
    return -(-4 * PIECES * experts // LANES) * LANES


def pack_kernel(caps, routes_in, probs_in, old_in, new_in, tokens, *refs):
    outs, refs = refs[: 2 * PIECES], refs[2 * PIECES :]
    slot_rows, routes, probs, old_place, new_place, sems = refs
    core, devices = lax.axis_index("tensor"), lax.axis_size("expert")
    width = tokens.shape[2]
    topk_count, token_count = routes.shape[1:]
    experts, slots = old_place.shape[0], new_place.shape[0]
    size = token_count // PIECES
    pairs = [(old_in, old_place), (new_in, new_place), (routes_in, routes), (probs_in, probs)]
    for i, out in enumerate(outs):
        batch = core if i < PIECES else 1 - core
        start = i % PIECES * size
        pairs.append((tokens.at[batch, start : start + size], out.at[:, :width]))
    copies = [pltpu.make_async_copy(src, dst, sems.at[i]) for i, (src, dst) in enumerate(pairs)]
    for copy in copies:
        copy.start()
    for copy in copies[:4]:
        copy.wait()
    slot = lax.broadcasted_iota(jnp.int32, (experts, token_count), 0)
    token = lax.broadcasted_iota(jnp.int32, (experts, token_count), 1)
    held, limit = jnp.zeros_like(slot), jnp.zeros_like(slot)
    for e in range(experts):
        held = jnp.where(slot == e, old_place[e], held)
        limit = jnp.where(slot == e, caps[1] * count_of(new_place, old_place[e], slots), limit)
    kinds = []
    for batch in (core, 1 - core):
        named, chance = routes[batch], probs[batch]
        weight = jnp.zeros((experts, token_count), jnp.float32)
        for k in range(topk_count):
            weight += jnp.where(named[k : k + 1] == held, chance[k : k + 1], 0.0)
        weight = jnp.where(token < jnp.where(batch == 0, caps[0], limit), weight, 0.0)
        high = weight.astype(jnp.bfloat16).astype(jnp.float32)
        kinds += [high, weight - high]
    lanes = side_lanes(experts)
    kinds.append(jnp.zeros((lanes - 4 * experts, token_count), jnp.float32))
    turned = jnp.concatenate(kinds, axis=0).T
    side = turned[:size]
    for i in range(1, PIECES):
        side += pltpu.roll(turned[i * size : (i + 1) * size], 4 * experts * i, 1)
    outs[PIECES - 1][:, width:] = side.astype(jnp.bfloat16)
    mine = slot_rows.shape[0]
    for j in range(mine):
        new_slot = lax.axis_index("expert") * mine + j
        expert = new_place[new_slot]
        holders = count_of(new_place, expert, slots)
        place = count_of(new_place, expert, new_slot)
        total = jnp.int32(0)
        for source in range(devices):
            start = lax.rem(place - source + devices * holders, holders)
            total += lax.div(token_count - 1 - start + holders, holders)
        slot_rows[j] = total
    for copy in copies[4:]:
        copy.wait()


def pack(caps, tokens, routes, probs, old_place, new_place):
    token_count, width = tokens.shape[1:]
    experts = old_place.shape[0]
    size = token_count // PIECES
    widths = [width] * (2 * PIECES)
    widths[PIECES - 1] += side_lanes(experts)
    routes, probs = routes.transpose(0, 2, 1), probs.transpose(0, 2, 1)
    mine = new_place.shape[0] // lax.axis_size("expert")
    vmem, smem = pl.BlockSpec(memory_space=pltpu.VMEM), pl.BlockSpec(memory_space=pltpu.SMEM)
    return pl.pallas_call(
        functools.partial(pack_kernel, caps),
        out_shape=[jax.ShapeDtypeStruct((size, w), tokens.dtype) for w in widths]
        + [jax.ShapeDtypeStruct((mine,), jnp.int32)],
        in_specs=[pl.BlockSpec(memory_space=pltpu.HBM)] * 5,
        out_specs=[vmem] * len(widths) + [smem],
        scratch_shapes=[
            pltpu.VMEM(routes.shape, routes.dtype),
            pltpu.VMEM(probs.shape, probs.dtype),
            pltpu.SMEM(old_place.shape, jnp.int32),
            pltpu.SMEM(new_place.shape, jnp.int32),
            pltpu.SemaphoreType.DMA((4 + len(widths),)),
        ],
        compiler_params=pltpu.CompilerParams(vmem_limit_bytes=VMEM_BYTES - (4 << 20)),
    )(routes, probs, old_place, new_place, tokens)


def half_of(core, half):
    return pl.ds(pl.multiple_of(core * half, LANES), half)


def expert_kernel(sides, outlets, width, experts, *refs):
    count = len(sides)
    rows, refs = refs[:count], refs[count:]
    (up_own, up_pair, down_own, down_pair), refs = refs[:4], refs[4:]
    outs, x_buf = list(refs[:-1]), refs[-1]
    slot, core = lax.axis_index("expert"), lax.axis_index("tensor")
    scales, place = [], 0
    for row, (holder, offset) in zip(rows, sides):
        x_buf[place : place + row.shape[0], :] = row[:, :width]
        place += row.shape[0]
        side = rows[holder][:, width:].astype(jnp.float32)
        lane = lax.broadcasted_iota(jnp.int32, side.shape, 1) - offset - slot
        mine = (lane == 0) | (lane == experts)
        scales.append(jnp.sum(jnp.where(mine, side, 0.0), axis=1, keepdims=True))
    scale = jnp.concatenate(scales, axis=0)
    x = x_buf[...]
    parts = []
    for up in (up_own, up_pair):
        v = jnp.dot(x, up[...], preferred_element_type=jnp.float32)
        parts.append((v / (1.0 + jnp.exp(-v))).astype(jnp.bfloat16))
    low = jnp.where(core == 0, parts[0], parts[1])
    high = jnp.where(core == 0, parts[1], parts[0])
    hidden = jnp.concatenate([low, high], axis=1)
    half = down_own.shape[1]
    groups = [[outs.pop(0) for _ in range(1 if held else 2)] for _, _, held in outlets]
    for j, down in enumerate((down_own, down_pair)):
        y = jnp.dot(hidden, down[...], preferred_element_type=jnp.float32)
        y = y.astype(jnp.bfloat16).astype(jnp.float32) * scale
        for (start, size, held), group in zip(outlets, groups):
            made = y[start : start + size]
            if held:
                columns = half_of(core if j == 0 else 1 - core, half)
                group[0][:, columns] = made.astype(held)
            else:
                group[j][...] = made.astype(group[j].dtype)


def expert_rows(hops, weights, width, experts, outlets):
    rows, sides = [], []
    for pieces in hops:
        holder = len(rows) + PIECES - 1
        for i in range(len(pieces)):
            chunk, piece = divmod(i, PIECES)
            sides.append((holder, (4 * piece + 2 * chunk) * experts))
        rows += pieces
    total = sum(row.shape[0] for row in rows)
    up = weights[0]
    vmem = pl.BlockSpec(memory_space=pltpu.VMEM)
    shapes = []
    for _, size, held in outlets:
        if held:
            shapes.append(((size, width), held))
        else:
            shapes += [((size, width // 2), t) for t in (jnp.float32, jnp.bfloat16)]
    return pl.pallas_call(
        functools.partial(expert_kernel, tuple(sides), outlets, width, experts),
        out_shape=[jax.ShapeDtypeStruct(*shape) for shape in shapes],
        in_specs=[vmem] * (len(rows) + 4),
        out_specs=[vmem] * len(shapes),
        scratch_shapes=[pltpu.VMEM((total, width), jnp.bfloat16)],
        compiler_params=pltpu.CompilerParams(vmem_limit_bytes=20 << 20),
        cost_estimate=pl.CostEstimate(
            flops=2 * total * width * 4 * up.shape[1],
            bytes_accessed=8 * total * width,
            transcendentals=2 * total * up.shape[1],
        ),
    )(*rows, *weights)


def split_add_kernel(part, arrived, goes_on, crosses):
    core, half = lax.axis_index("tensor"), crosses.shape[1]
    for out, which in ((goes_on, 1 - core), (crosses, core)):
        columns = half_of(which, half)
        out[...] = (part[:, columns] + arrived[:, columns].astype(jnp.float32)).astype(out.dtype)


def split_add(part, arrived):
    size, half = part.shape[0], part.shape[1] // 2
    vmem = pl.BlockSpec(memory_space=pltpu.VMEM)
    return pl.pallas_call(
        split_add_kernel,
        out_shape=[jax.ShapeDtypeStruct((size, half), jnp.bfloat16)] * 2,
        in_specs=[vmem, vmem],
        out_specs=[vmem, vmem],
        compiler_params=pltpu.CompilerParams(vmem_limit_bytes=4 << 20),
    )(part, arrived)


def other_half_kernel(x, out):
    out[...] = x[:, half_of(1 - lax.axis_index("tensor"), out.shape[1])]


def other_half(x):
    vmem = pl.BlockSpec(memory_space=pltpu.VMEM)
    return pl.pallas_call(
        other_half_kernel,
        out_shape=jax.ShapeDtypeStruct((x.shape[0], x.shape[1] // 2), x.dtype),
        in_specs=[vmem],
        out_specs=vmem,
        compiler_params=pltpu.CompilerParams(vmem_limit_bytes=4 << 20),
    )(x)


def finish_kernel(pieces, own, own_pair, *refs):
    arrived, second_pair, second, crossed = (refs[i * pieces : (i + 1) * pieces] for i in range(4))
    result, mixed, sems = refs[-3:]
    core = lax.axis_index("tensor")
    half = mixed.shape[2]
    size = own.shape[0] // pieces
    f32 = jnp.float32
    copies = []
    for i in range(pieces):
        rows = slice(i * size, (i + 1) * size)
        total = own[rows] + arrived[i][...].astype(f32) + second_pair[i][...].astype(f32)
        mixed[core, rows] = total.astype(mixed.dtype)
        total = second[i][:, half_of(core, half)].astype(f32) + crossed[i][...].astype(f32)
        mixed[1 - core, rows] = (total + own_pair[rows].astype(f32)).astype(mixed.dtype)
        piece = mixed.at[:, rows], result.at[:, rows]
        copies.append(pltpu.make_async_copy(*piece, sems.at[i]))
        copies[-1].start()
    for copy in copies:
        copy.wait()


def finish(pieces, own, own_pair, *groups):
    vmem = pl.BlockSpec(memory_space=pltpu.VMEM)
    return pl.pallas_call(
        functools.partial(finish_kernel, pieces),
        out_shape=jax.ShapeDtypeStruct((2, *own.shape), jnp.bfloat16),
        in_specs=[vmem] * (2 + 4 * pieces),
        out_specs=pl.BlockSpec(memory_space=pltpu.HBM),
        scratch_shapes=[
            pltpu.VMEM((2, *own.shape), jnp.bfloat16),
            pltpu.SemaphoreType.DMA((pieces,)),
        ],
        compiler_params=pltpu.CompilerParams(vmem_limit_bytes=4 << 20),
    )(own, own_pair, *sum((list(g) for g in groups), []))


def by_ring(ring, tokens, routes, probs, up_weight, down_weight, old_place, new_place):
    devices = lax.axis_size("expert")
    token_count, width = tokens.shape[1], tokens.shape[2]
    experts = old_place.shape[0]
    block_rows = token_count * routes.shape[2]
    both = ("expert", "tensor")
    steps = devices // 2
    ahead = []
    for spot, here in enumerate(ring):
        there = ring[(spot + 1) % devices]
        core, next_core = spot % 2, (spot + 1) % 2
        ahead.append((2 * here + core, 2 * there + next_core))
        ahead.append((2 * there + 1 - next_core, 2 * here + 1 - core))
    back = [(b, a) for a, b in ahead]
    across = [(b, a ^ 1) for a, b in ahead]
    swap = [(0, 1), (1, 0)]
    f32, bf16 = jnp.float32, jnp.bfloat16
    each = range(PIECES)
    size = token_count // PIECES

    caps = (
        capacity_for(block_rows, experts, token_count),
        capacity_for(block_rows, new_place.shape[0], token_count),
    )
    *packed, slot_rows = pack(caps, tokens, routes, probs, old_place, new_place)
    first, second = [packed[:PIECES]], [packed[PIECES:]]
    for step in range(1, steps + 1):
        first.append([lax.ppermute(first[-1][i], both, ahead) for i in each])
        if step < steps:
            second.append([lax.ppermute(second[-1][i], both, ahead) for i in each])
    up_own, down_own = up_weight[0], down_weight[0]
    up_pair = lax.ppermute(up_own, "tensor", swap)
    down_pair = lax.ppermute(down_own, "tensor", swap)
    up_here = lax.ppermute(up_pair, "tensor", swap)
    down_here = lax.ppermute(down_pair, "tensor", swap)
    weights = (up_here, up_pair, down_here, down_pair)

    def run(held, outlets):
        return expert_rows(held, weights, width, experts, outlets)

    def ranges(chunk, held):
        return [(chunk * token_count + i * size, size, held) for i in each]

    part_first, part_second = [None] * steps, [None] * steps
    own, leaving, *made = run(
        [first[0], first[1] + second[1]], [(0, token_count, None), *ranges(1, f32), *ranges(2, f32)]
    )
    part_first[1], part_second[1] = made[:PIECES], made[PIECES:]
    for step in range(2, steps):
        made = run(
            [first[step] + second[step]],
            ranges(0, f32) + ranges(1, bf16 if step == steps - 1 else f32),
        )
        part_first[step], part_second[step] = made[:PIECES], made[PIECES:]
    sum_first = run([first[steps]], ranges(0, bf16))
    sum_second = part_second[steps - 1]
    own_pair = lax.ppermute(leaving, "tensor", swap)

    for step in range(steps - 2, -1, -1):
        sum_second = [lax.ppermute(sum_second[i], both, back) for i in each]
        if step > 0:
            sum_second = [
                (part + arrived.astype(f32)).astype(bf16)
                for part, arrived in zip(part_second[step], sum_second)
            ]
    second_pair = [lax.ppermute(other_half(sum_second[i]), "tensor", swap) for i in each]
    for step in range(steps - 1, 1, -1):
        sum_first = [lax.ppermute(sum_first[i], both, back) for i in each]
        sum_first = [
            (part + arrived.astype(f32)).astype(bf16)
            for part, arrived in zip(part_first[step], sum_first)
        ]
    arrived, crossed = [], []
    for i in each:
        last = lax.ppermute(sum_first[i], both, back)
        stays, crosses = split_add(part_first[1][i], last)
        arrived.append(lax.ppermute(stays, both, back))
        crossed.append(lax.ppermute(crosses, both, across))
    mixed = finish(PIECES, own, own_pair, arrived, second_pair, sum_second, crossed)
    return (mixed, slot_rows)


def on_device(ring, tokens, routes, probs, up_weight, down_weight, old_place, new_place):
    devices = lax.axis_size("expert")
    experts = old_place.shape[0]
    arrays = (tokens, routes, probs, up_weight, down_weight, old_place, new_place)
    if (
        experts == routes.shape[2]
        and experts == devices
        and devices >= 6
        and devices % 2 == 0
        and lax.axis_size("tensor") == 2
        and tokens.shape[0] == 2
        and tokens.shape[1] % (SUBLANES * PIECES) == 0
    ):
        return by_ring(ring, *arrays)
    return by_capacity(*arrays)


def solution(mesh):
    placed = (
        P(None, ("groups", "expert"), None),
        P(None, ("groups", "expert"), None),
        P(None, ("groups", "expert"), None),
        P("expert", None, "tensor"),
        P("expert", None, "tensor"),
        P("groups"),
        P("groups"),
    )
    return jax.shard_map(
        functools.partial(on_device, ring_order(mesh)),
        mesh=mesh,
        in_specs=placed,
        out_specs=(P(None, ("groups", "expert"), "tensor"), P(("groups", "expert"))),
        check_vma=False,
    )
```
